256 devices in a mesh: seq: 64 (over z, y, core), head: 4 (over x).
Axes of the slice: x: 4, y: 4, z: 8, core: 2. Of those that a mesh axis runs over, the one named last changes fastest.
Arguments:
- query_raw: bfloat16 [16384, 5120], P('seq', 'head'), may hold values from -200 to 200
- key_raw: bfloat16 [16384, 5120], P('seq', 'head'), may hold values from -200 to 200
- values: bfloat16 [16384, 5120], P('seq', 'head'), may hold values from -6 to 6
- grad_out: bfloat16 [16384, 5120], P('seq', 'head'), may hold values from -18 to 18
- query_gain: bfloat16 [5120], P('head'), may hold values from 0.25 to 1.75
- key_gain: bfloat16 [5120], P('head'), may hold values from 0.25 to 1.75
- cluster_of: int32 [16384], P('seq'), may hold values from 0 to 255, as said below
- pair_mask: int32 [256, 256], replicated, may hold values from 0 to 1, as said below
- cluster_owner: int32 [256], replicated, may hold values from 0 to 63, as said below
Outputs:
- grad_query: bfloat16 [16384, 5120], P('seq', 'head')
- grad_key: bfloat16 [16384, 5120], P('seq', 'head')
- grad_values: bfloat16 [16384, 5120], P('seq', 'head')
The draws below stay inside these ranges and needn't reach their ends.
Inputs may be any that keep to these rules, and one draw needn't show every extreme that they name: `cluster_of`: at most 2 of the 256 tokens of one seq index lie in one cluster. `cluster_owner`: every index along seq owns exactly 4 clusters. `pair_mask`: 1 on the diagonal; 0 between clusters of different owners.
All inputs are finite; a program needn't handle non-finite values.
Results may differ from the reference program's by a relative error of at most 0.011.
Values may be sent and summed in bfloat16 or wider, within the bound.
No kernel may reach another device: no remote copies, remote signals or barrier semaphores. Data moves between devices by JAX's collectives and lax.ppermute only.
A program may use at most 128 MiB of HBM per device.

```python
import math
import jax
import jax.numpy as jnp
from jax import lax

WIDTH = 5120
HEADS = 40
HEAD_DIM = 128
TOK_DEV = 256
OWNED = 4
CLUSTERS = 256
SOURCE_CAP = 2
TOKENS = 16384
N_SEQ = 64


def cluster_table(key):
    slots_all = CLUSTERS * SOURCE_CAP
    block_count = TOKENS // TOK_DEV
    full_cluster = jax.random.randint(jax.random.fold_in(key, 11), (), 0, CLUSTERS)
    block_keys = jax.random.split(jax.random.fold_in(key, 12), block_count)
    slot_cluster = jnp.arange(slots_all, dtype=jnp.int32) // SOURCE_CAP

    def one_block(block_key):
        first_key, second_key, third_key = jax.random.split(block_key, 3)
        second_cluster = (full_cluster + 1 + jax.random.randint(first_key, (), 0, CLUSTERS - 1)) % CLUSTERS
        order_rank = jax.random.permutation(second_key, slots_all).astype(jnp.int32)
        forced = (slot_cluster == full_cluster) | (slot_cluster == second_cluster)
        priority = order_rank + slots_all * (1 - forced.astype(jnp.int32))
        chosen = slot_cluster[jnp.argsort(priority)[:TOK_DEV]]
        return chosen[jax.random.permutation(third_key, TOK_DEV)]
    return jax.vmap(one_block)(block_keys).reshape(-1).astype(jnp.int32)


def owner_table(key):
    return (jax.random.permutation(jax.random.fold_in(key, 21), CLUSTERS) // OWNED).astype(jnp.int32)


def draw_cluster_of(key, part):
    return cluster_table(key)


def draw_cluster_owner(key, part):
    return owner_table(key)


def draw_pair_mask(key, part):
    owners = owner_table(key)
    level = jax.random.randint(jax.random.fold_in(key, 31), (CLUSTERS // OWNED,), 0, 5)
    coin = jax.random.randint(jax.random.fold_in(key, 32), (CLUSTERS, CLUSTERS), 0, 4)
    same_owner = owners[:, None] == owners[None, :]
    dense_pair = coin < level[owners][:, None]
    diagonal = jnp.arange(CLUSTERS)[:, None] == jnp.arange(CLUSTERS)[None, :]
    return jnp.where(diagonal | same_owner & dense_pair, 1, 0).astype(jnp.int32)


def projection_side(side_key):
    col_key, row_key, noise_key = jax.random.split(side_key, 3)
    position = jnp.arange(WIDTH, dtype=jnp.float32) / WIDTH
    column_scale = jnp.exp(jax.random.uniform(col_key, (WIDTH,), minval=0.0, maxval=math.log(10.0)))
    row_scale = jnp.exp(jax.random.uniform(row_key, (TOKENS, 1), minval=math.log(0.3), maxval=math.log(3.0)))
    noise = jnp.clip(jax.random.normal(noise_key, (TOKENS, WIDTH)), -5.0, 5.0)
    base = 0.15 * column_scale * (1.0 + 0.8 * position) * noise
    return base * row_scale


def query_key_pair(key):
    query_full = projection_side(jax.random.fold_in(key, 41))
    key_full = projection_side(jax.random.fold_in(key, 42))
    return (query_full, key_full)


def draw_query_raw(key, part):
    return query_key_pair(key)[0].astype(jnp.bfloat16)


def draw_key_raw(key, part):
    return query_key_pair(key)[1].astype(jnp.bfloat16)


def block_levels(rng, extent, shards, smallest, largest):
    def one(dim, parts):
        draws = jax.random.uniform(jax.random.fold_in(jax.random.fold_in(rng, 6), dim), (parts,), jnp.float32, smallest / len(shards), largest / len(shards))
        return jnp.repeat(jnp.exp(draws), extent[dim] // parts).reshape((-1,) + (1,) * (len(extent) - dim - 1))

    gain = one(*shards[0])
    for cut in shards[1:]:
        gain = gain * one(*cut)
    return gain


def centred(own_key, extent, scale, reach, cuts=(), kind=jnp.bfloat16):
    loudness = block_levels(own_key, extent, cuts, -0.22, 0.18) if cuts else 1.0
    drawn = jax.random.normal(own_key, extent, jnp.float32) * scale * loudness
    return jnp.minimum(jnp.maximum(drawn, -reach), reach).astype(kind)


def setup_inputs(seed: int = 0) -> dict:
    keys = jax.random.split(jax.random.key(seed), 10)
    return {
        "query_raw": draw_query_raw(jax.random.fold_in(keys[9], 71), 0),
        "key_raw": draw_key_raw(jax.random.fold_in(keys[9], 71), 0),
        "values": centred(keys[2], (TOKENS, WIDTH), 1.0, 6.0, ((0, 64), (1, 4))),
        "grad_out": centred(keys[3], (TOKENS, WIDTH), 3.0, 18.0, ((0, 64), (1, 4))),
        "query_gain": jnp.clip(1.0 + 0.15 * jax.random.normal(keys[4], (WIDTH,), jnp.float32), 0.25, 1.75).astype(jnp.bfloat16),
        "key_gain": jnp.clip(1.0 + 0.15 * jax.random.normal(keys[5], (WIDTH,), jnp.float32), 0.25, 1.75).astype(jnp.bfloat16),
        "cluster_of": draw_cluster_of(jax.random.fold_in(keys[9], 71), 0),
        "pair_mask": draw_pair_mask(jax.random.fold_in(keys[9], 71), 0),
        "cluster_owner": draw_cluster_owner(jax.random.fold_in(keys[9], 71), 0),
    }


EPSILON = 1e-06
NEGATIVE = -1e+30

def widen(array):
    return lax.optimization_barrier(array).astype(jnp.float32)

def norm_scale(unnormed):
    return jnp.sqrt(lax.optimization_barrier(jnp.sum(jnp.square(unnormed.astype(jnp.float32)), axis=1)) / WIDTH + EPSILON)

def normalize(unnormed, gain_vector, row_scale):
    return (unnormed.astype(jnp.float32) * gain_vector.astype(jnp.float32)[None, :] / row_scale[:, None]).astype(jnp.bfloat16)

def norm_grad(grad_norm, unnormed, gain_vector, row_scale):
    lifted = grad_norm.astype(jnp.float32) * gain_vector.astype(jnp.float32)[None, :]
    inner_sum = lax.optimization_barrier(jnp.sum(lifted * unnormed.astype(jnp.float32), axis=1))
    result = lifted / row_scale[:, None] - unnormed.astype(jnp.float32) * (inner_sum / (WIDTH * row_scale ** 3))[:, None]
    return result.astype(jnp.bfloat16)

def attend_block(query_tiles, key_tiles, value_tiles, grad_tiles, live_slots, local_mask):
    sources, clusters_here, per_source, head_count, head_size = query_tiles.shape
    capacity = sources * per_source
    query_wide = widen(query_tiles)
    key_wide = widen(key_tiles)
    value_wide = value_tiles.astype(jnp.float32)
    grad_wide = grad_tiles.astype(jnp.float32)
    scores = jnp.einsum('scmhe,tbnhe->hcsmbtn', query_wide, key_wide)
    scores = scores.reshape(head_count, clusters_here, capacity, clusters_here, capacity) / math.sqrt(head_size)
    allowed = (local_mask[:, None, :, None] > 0.5) & live_slots[:, :, None, None] & live_slots[None, None, :, :]
    row_max = lax.optimization_barrier(jnp.max(jnp.where(allowed[None], scores, NEGATIVE), axis=(3, 4), keepdims=True))
    raised = jnp.where(allowed[None], jnp.exp(scores - row_max), 0.0)
    row_total = lax.optimization_barrier(jnp.sum(raised, axis=(3, 4), keepdims=True))
    row_total = jnp.where(live_slots[None, :, :, None, None], row_total, 1.0)
    seven_dims = (head_count, clusters_here, sources, per_source, clusters_here, sources, per_source)
    weights_full = (raised / row_total).reshape(seven_dims)
    weights_low = widen(weights_full.astype(jnp.bfloat16))
    attended = jnp.einsum('hcsmbtn,tbnhe->scmhe', weights_low, value_wide)
    delta_rows = lax.optimization_barrier(jnp.sum(grad_wide * attended, axis=4))
    delta_rows = jnp.transpose(delta_rows, (3, 1, 0, 2))[:, :, :, :, None, None, None]
    grad_probs = jnp.einsum('scmhe,tbnhe->hcsmbtn', grad_wide, value_wide)
    grad_scores = widen((weights_full * (grad_probs - delta_rows) / math.sqrt(head_size)).astype(jnp.bfloat16))
    grad_value = jnp.einsum('hcsmbtn,scmhe->tbnhe', weights_low, grad_wide).astype(jnp.bfloat16)
    grad_query = jnp.einsum('hcsmbtn,tbnhe->scmhe', grad_scores, key_wide).astype(jnp.bfloat16)
    grad_keys = jnp.einsum('hcsmbtn,scmhe->tbnhe', grad_scores, query_wide).astype(jnp.bfloat16)
    return (grad_value, grad_query, grad_keys)

def reference(query_raw, key_raw, values, grad_out, query_gain, key_gain, cluster_of, pair_mask, cluster_owner):
    scale_q = norm_scale(query_raw)
    scale_k = norm_scale(key_raw)
    q_norm = normalize(query_raw, query_gain, scale_q)
    k_norm = normalize(key_raw, key_gain, scale_k)
    cluster_ids = jnp.arange(CLUSTERS, dtype=jnp.int32)
    same_owner = cluster_owner[:, None] == cluster_owner[None, :]
    local_index = lax.optimization_barrier(jnp.sum((same_owner & (cluster_ids[None, :] < cluster_ids[:, None])).astype(jnp.int32), axis=1)).astype(jnp.int32)
    blocks = cluster_of.reshape(N_SEQ, TOK_DEV)
    token_ids = jnp.arange(TOK_DEV, dtype=jnp.int32)
    earlier = token_ids[None, None, :] < token_ids[None, :, None]
    token_rank = lax.optimization_barrier(jnp.sum(((blocks[:, :, None] == blocks[:, None, :]) & earlier).astype(jnp.int32), axis=2)).reshape(-1).astype(jnp.int32)
    source = (jnp.arange(TOKENS, dtype=jnp.int32) // TOK_DEV).astype(jnp.int32)
    target = cluster_owner[cluster_of].astype(jnp.int32)
    slots = N_SEQ * OWNED * SOURCE_CAP
    global_slot = (((target * N_SEQ + source) * OWNED + local_index[cluster_of]) * SOURCE_CAP + token_rank).astype(jnp.int32)
    slot_table = jnp.full((N_SEQ * slots,), TOKENS, dtype=jnp.int32).at[global_slot].set(jnp.arange(TOKENS, dtype=jnp.int32))

    def padded(array):
        return jnp.concatenate([array, jnp.zeros((1, WIDTH), array.dtype)], axis=0)
    query_pad = padded(q_norm)
    key_pad = padded(k_norm)
    value_pad = padded(values)
    grad_pad = padded(grad_out)
    mask_float = pair_mask.astype(jnp.float32)
    tile_shape = (N_SEQ, OWNED, SOURCE_CAP, HEADS, HEAD_DIM)

    def per_owner(owner_id):
        slot_tokens = lax.dynamic_slice_in_dim(slot_table, (owner_id * slots).astype(jnp.int32), slots)
        live_slots = jnp.transpose((slot_tokens < TOKENS).reshape(N_SEQ, OWNED, SOURCE_CAP), (1, 0, 2)).reshape(OWNED, N_SEQ * SOURCE_CAP)
        selector = ((cluster_owner[None, :] == owner_id) & (local_index[None, :] == jnp.arange(OWNED, dtype=jnp.int32)[:, None])).astype(jnp.float32)
        local_mask = jnp.dot(jnp.dot(selector, mask_float, precision=lax.Precision.HIGHEST), selector.T, precision=lax.Precision.HIGHEST)
        grad_value, grad_query, grad_keys = attend_block(query_pad[slot_tokens].reshape(tile_shape), key_pad[slot_tokens].reshape(tile_shape), value_pad[slot_tokens].reshape(tile_shape), grad_pad[slot_tokens].reshape(tile_shape), live_slots, local_mask)
        return (grad_query.reshape(slots, WIDTH), grad_keys.reshape(slots, WIDTH), grad_value.reshape(slots, WIDTH))
    owner_parts = lax.map(per_owner, jnp.arange(N_SEQ, dtype=jnp.int32))
    grad_qn = owner_parts[0].reshape(-1, WIDTH)[global_slot]
    grad_kn = owner_parts[1].reshape(-1, WIDTH)[global_slot]
    grad_values = owner_parts[2].reshape(-1, WIDTH)[global_slot]
    grad_query = norm_grad(grad_qn, query_raw, query_gain, scale_q)
    grad_key = norm_grad(grad_kn, key_raw, key_gain, scale_k)
    return (grad_query, grad_key, grad_values)
```

```python
import functools
import math

import jax
import jax.numpy as jnp
from jax import lax
from jax.experimental import pallas as pl
from jax.experimental.pallas import tpu as pltpu
from jax.sharding import PartitionSpec as P


WIDTH = 5120
HEAD_DIM = 128
EPSILON = 1e-06
NEGATIVE = -1e30

TOK = 256
NZ = 8
NR = 8
OWNED = 4
SRC_CAP = 48
Y_CAP = 64
Z_CAP = 56
SRC_ROWS = NZ * SRC_CAP
WIDTH_HERE = 1280
HEADS_HERE = 10
HEADS_A = 5
LANES = 128


Y_GROUPS = [[NR * z + r for r in range(NR)] for z in range(NZ)]


def z_perm(shift):
    return [(s, ((s // NR + shift) % NZ) * NR + s % NR) for s in range(NZ * NR)]


def head_perm(shift):
    return [(s, (s + shift) % 4) for s in range(4)]


def call(body, out_shape, flops=0, moved=0, scratch=()):
    return pl.pallas_call(
        body,
        out_shape=out_shape,
        scratch_shapes=scratch,
        cost_estimate=pl.CostEstimate(flops=flops, bytes_accessed=moved, transcendentals=0),
        compiler_params=pltpu.CompilerParams(vmem_limit_bytes=48 * 1024 * 1024),
    )


def iota(shape, dim):
    return lax.broadcasted_iota(jnp.int32, shape, dim)


def to_col(row):
    n = row.shape[1]
    eye = iota((n, n), 0) == iota((n, n), 1)
    return jnp.sum(jnp.where(eye, jnp.broadcast_to(row, (n, n)), jnp.zeros((), row.dtype)), axis=1, keepdims=True)


def to_row(col):
    n = col.shape[0]
    eye = iota((n, n), 0) == iota((n, n), 1)
    return jnp.sum(jnp.where(eye, jnp.broadcast_to(col, (n, n)), jnp.zeros((), col.dtype)), axis=0, keepdims=True)


def mm(a, b, dims):
    return lax.dot_general(a, b, (dims, ((), ())), preferred_element_type=jnp.float32)


def prep_body(cluster_ref, owner_ref, z_ref, table_ref, code_ref, dest_a_ref, dest_b_ref):
    square = (TOK, TOK)
    owner_row = owner_ref[...]
    owner_col = to_col(owner_row)
    earlier = iota(square, 0) < iota(square, 1)
    one, zero = jnp.int32(1), jnp.int32(0)
    local_row = jnp.sum(
        jnp.where((owner_col == owner_row) & earlier, one, zero), axis=0, keepdims=True
    )
    table_row = owner_row * OWNED + local_row
    table_ref[...] = table_row
    table_col = to_col(table_row)
    code_row = jnp.sum(
        jnp.where(iota(square, 0) == cluster_ref[...], table_col, zero), axis=0, keepdims=True
    )
    code_ref[...] = code_row
    for key_row, out_ref in (
        (((code_row >> 5) - z_ref[0] + NZ) & (NZ - 1), dest_a_ref),
        ((code_row >> 2) & (NR - 1), dest_b_ref),
    ):
        key_col = to_col(key_row)
        rank_row = jnp.sum(
            jnp.where((key_col == key_row) & earlier, one, zero), axis=0, keepdims=True
        )
        out_ref[...] = jnp.where(rank_row < SRC_CAP, key_row * SRC_CAP + rank_row, -1)


VMEM_SPEC = pl.BlockSpec(memory_space=pltpu.VMEM)
SMEM_SPEC = pl.BlockSpec(memory_space=pltpu.SMEM)


def prep(cluster_of, cluster_owner, z_here):
    row = jax.ShapeDtypeStruct((1, TOK), jnp.int32)
    return pl.pallas_call(
        prep_body,
        out_shape=(row,) * 4,
        in_specs=[VMEM_SPEC, VMEM_SPEC, SMEM_SPEC],
        out_specs=(VMEM_SPEC,) * 4,
        name="prep",
    )(cluster_of.reshape(1, TOK), cluster_owner.reshape(1, TOK), z_here.reshape(1))


def mask_body(table_ref, mask_ref, own_ref, out_ref):
    slots = iota((LANES, TOK), 0)
    chosen = (table_ref[...] == own_ref[0] * OWNED + slots) & (slots < OWNED)
    chosen = jnp.where(chosen, 1.0, 0.0).astype(jnp.bfloat16)
    pairs = mask_ref[...].astype(jnp.float32).astype(jnp.bfloat16)
    rows = mm(chosen, pairs, ((1,), (0,))).astype(jnp.bfloat16)
    out_ref[...] = mm(rows, chosen, ((1,), (1,))).astype(jnp.bfloat16)


def small_mask(table_row, pair_mask, own_index):
    return pl.pallas_call(
        mask_body,
        out_shape=jax.ShapeDtypeStruct((LANES, LANES), jnp.bfloat16),
        in_specs=[VMEM_SPEC, VMEM_SPEC, SMEM_SPEC],
        out_specs=VMEM_SPEC,
        name="mask",
    )(table_row, pair_mask, own_index.reshape(1))


def bias_of(code, small):
    local = jnp.where(code > 0, (code - 1) & (OWNED - 1), -1)
    hot = jnp.where(local == iota(local.shape, 1), 1.0, 0.0).astype(jnp.bfloat16)
    reach = mm(hot, small, ((1,), (1,))).astype(jnp.bfloat16)
    return jnp.where(mm(reach, hot, ((1,), (1,))) > 0.5, 0.0, NEGATIVE)


def overflow_count(codes):
    def over(keys, count, cap):
        hit = keys[:, None, :] == jnp.arange(count, dtype=jnp.int32)[None, :, None]
        return (jnp.max(jnp.sum(hit.astype(jnp.int32), axis=2)) > cap).astype(jnp.int32)

    planes = codes.reshape(NZ, NR * TOK) >> 2
    return jnp.maximum(
        jnp.maximum(over(codes >> 5, NZ, SRC_CAP), over((codes >> 2) & (NR - 1), NR, SRC_CAP)),
        over(planes, NZ * NR, Z_CAP),
    )


def squares_body(q_ref, k_ref, out_ref):
    q = q_ref[...].astype(jnp.float32)
    k = k_ref[...].astype(jnp.float32)
    out_ref[0:1, :] = to_row(jnp.sum(q * q, axis=1, keepdims=True))
    out_ref[1:2, :] = to_row(jnp.sum(k * k, axis=1, keepdims=True))
    out_ref[2:8, :] = jnp.zeros((6, TOK), jnp.float32)


def over_head(part):
    return [part] + [lax.ppermute(part, "head", head_perm(d)) for d in (1, 2, 3)]


def total_of(refs):
    return (refs[0][...] + refs[1][...]) + (refs[2][...] + refs[3][...])


def scale_col(total, which):
    return jnp.sqrt(to_col(total[which : which + 1, :]) / WIDTH + EPSILON)


def place_rows(dest_row):
    return jnp.where(iota((SRC_ROWS, TOK), 0) == dest_row, 1.0, 0.0).astype(jnp.bfloat16)


def store_blocks(outs, packed, start):
    width = packed.shape[1]
    cap = packed.shape[0] // len(outs)
    for d, out in enumerate(outs):
        out[:, start : start + width] = packed[d * cap : (d + 1) * cap, :]


def normed(raw, gain, scale):
    return (raw.astype(jnp.float32) * gain.astype(jnp.float32) / scale).astype(jnp.bfloat16)


def pack_body(lo, hi, dest_ref, code_ref, v_ref, g_ref, q_ref, k_ref, qg_ref, kg_ref, *refs):
    total = total_of(refs[:4])
    outs = refs[4:]
    hot = place_rows(dest_ref[...])
    cols = slice(lo * HEAD_DIM, hi * HEAD_DIM)
    width = (hi - lo) * HEAD_DIM
    code = jnp.broadcast_to(to_col(code_ref[...]) + 1, (TOK, LANES))
    code = code.astype(jnp.float32).astype(jnp.bfloat16)
    parts = [v_ref[:, cols], g_ref[:, cols]]
    for which, (ref, gain) in enumerate(((q_ref, qg_ref), (k_ref, kg_ref))):
        parts.append(normed(ref[:, cols], gain[:, cols], scale_col(total, which)))
    parts.append(code)
    for n, part in enumerate(parts):
        store_blocks(outs, mm(hot, part, ((1,), (0,))).astype(jnp.bfloat16), n * width)


def blocks_of(count, rows, width):
    return (jax.ShapeDtypeStruct((rows, width), jnp.bfloat16),) * count


def pack(lo, hi, count, args):
    width = (hi - lo) * HEAD_DIM * 4 + LANES
    return call(
        functools.partial(pack_body, lo, hi),
        blocks_of(count, SRC_ROWS // count, width),
        flops=2 * SRC_ROWS * TOK * width,
        moved=4 * SRC_ROWS * width,
    )(*args)


def z_exchange(blocks, sign):
    return [blocks[0]] + [
        lax.ppermute(blocks[d], "seq", z_perm(sign * d)) for d in range(1, NZ)
    ]


def y_exchange(rows):
    return lax.all_to_all(
        rows, "seq", split_axis=0, concat_axis=0, axis_index_groups=Y_GROUPS, tiled=True
    )


def stacked(blocks, cols):
    if len(blocks) == 1:
        return blocks[0][:, cols]
    return jnp.concatenate([b[:, cols] for b in blocks], axis=0)


def steps_of(width):
    return [slice(a, min(a + 512, width)) for a in range(0, width, 512)]


def spread_body(mode, count_in, cap, z_ref, *refs):
    blocks, outs, table_ref = refs[:count_in], refs[count_in:-1], refs[-1]
    width = outs[0].shape[1]
    code = stacked(blocks, slice(width - LANES, width)).astype(jnp.float32).astype(jnp.int32)
    code = code[:, 0:1]
    if mode == "y":
        key = ((code - 1) >> 2) & (NR - 1)
    else:
        key = (((code - 1) >> 5) - z_ref[0] + NZ) & (NZ - 1)
    key_col = jnp.where(code > 0, key, -1)
    key_row = to_row(key_col)
    square = (SRC_ROWS, SRC_ROWS)
    before = (key_col == key_row) & (iota(square, 0) < iota(square, 1))
    rank_row = jnp.sum(jnp.where(before, jnp.int32(1), jnp.int32(0)), axis=0, keepdims=True)
    dest = jnp.where((key_row >= 0) & (rank_row < cap), key_row * cap + rank_row, -1)
    table_ref[...] = dest
    hot = jnp.where(iota((NZ * cap, SRC_ROWS), 0) == dest, 1.0, 0.0).astype(jnp.bfloat16)
    for cols in steps_of(width):
        packed = mm(hot, stacked(blocks, cols), ((1,), (0,))).astype(jnp.bfloat16)
        store_blocks(outs, packed, cols.start)


def spread(mode, blocks, count_out, cap, z_here):
    width = blocks[0].shape[1]
    outs = pl.pallas_call(
        functools.partial(spread_body, mode, len(blocks), cap),
        out_shape=blocks_of(count_out, NZ * cap // count_out, width)
        + (jax.ShapeDtypeStruct((1, SRC_ROWS), jnp.int32),),
        in_specs=[SMEM_SPEC] + [VMEM_SPEC] * len(blocks),
        out_specs=(VMEM_SPEC,) * (count_out + 1),
        cost_estimate=pl.CostEstimate(
            flops=2 * NZ * cap * SRC_ROWS * width, bytes_accessed=0, transcendentals=0
        ),
        compiler_params=pltpu.CompilerParams(vmem_limit_bytes=48 * 1024 * 1024),
    )(z_here.reshape(1), *blocks)
    return outs[:-1], outs[-1]


def gather_body(count_in, cap, table_ref, *refs):
    blocks, outs = refs[:count_in], refs[count_in:]
    hot = jnp.where(iota((NZ * cap, SRC_ROWS), 0) == table_ref[...], 1.0, 0.0).astype(jnp.bfloat16)
    for cols in steps_of(outs[0].shape[1]):
        packed = mm(hot, stacked(blocks, cols), ((0,), (0,))).astype(jnp.bfloat16)
        store_blocks(outs, packed, cols.start)


def gather(table, blocks, count_out, cap):
    width = blocks[0].shape[1]
    return call(
        functools.partial(gather_body, len(blocks), cap),
        blocks_of(count_out, SRC_ROWS // count_out, width),
        flops=2 * NZ * cap * SRC_ROWS * width,
        moved=4 * NZ * cap * width,
    )(table, *blocks)


def inner_row(grad, raw, gain):
    lifted = grad.astype(jnp.float32) * gain.astype(jnp.float32)
    return to_row(jnp.sum(lifted * raw.astype(jnp.float32), axis=1, keepdims=True))


def unpack_body(lo, hi, dest_ref, q_ref, k_ref, qg_ref, kg_ref, *refs):
    blocks, outs, inner_ref = refs[:-4], refs[-4:-1], refs[-1]
    hot = place_rows(dest_ref[...])
    width = outs[0].shape[1]
    cols = slice(lo * HEAD_DIM, hi * HEAD_DIM)
    sides = (None, (q_ref, qg_ref), (k_ref, kg_ref))
    for n, (out, side) in enumerate(zip(outs, sides)):
        rows = stacked(blocks, slice(n * width, (n + 1) * width))
        grad = mm(hot, rows, ((0,), (0,))).astype(jnp.bfloat16)
        out[...] = grad
        if side is not None:
            inner_ref[n - 1 : n, :] = inner_row(grad, side[0][:, cols], side[1][:, cols])
    inner_ref[2:8, :] = jnp.zeros((6, TOK), jnp.float32)


def unpack(lo, hi, dest, sides, blocks):
    width = (hi - lo) * HEAD_DIM
    return call(
        functools.partial(unpack_body, lo, hi),
        blocks_of(3, TOK, width) + (jax.ShapeDtypeStruct((8, TOK), jnp.float32),),
        flops=2 * SRC_ROWS * TOK * width * 3,
        moved=4 * SRC_ROWS * width * 3,
    )(dest, *sides, *blocks)


def attend_body(heads, count, small_ref, *refs):
    blocks, outs = refs[:count], refs[count : 2 * count]
    bias_ref, probs_ref, grads_ref = refs[2 * count : 2 * count + 3]
    rows, width = bias_ref.shape[0], heads * HEAD_DIM
    if count == 1:
        data, result = blocks[0], outs[0]
    else:
        data, result = refs[2 * count + 3 :]
        cap = rows // count
        for d, block in enumerate(blocks):
            data[d * cap : (d + 1) * cap, :] = block[...]
    inv = 1.0 / math.sqrt(HEAD_DIM)
    code = data[:, 4 * width : 4 * width + LANES].astype(jnp.float32).astype(jnp.int32)
    bias_ref[...] = bias_of(code, small_ref[...])

    def one_head(h, carry):
        v_ref, g_ref, q_ref, k_ref = (
            data.at[:, pl.ds(pl.multiple_of(n * width + h * HEAD_DIM, HEAD_DIM), HEAD_DIM)]
            for n in range(4)
        )
        keys = k_ref[...]
        vals = v_ref[...]
        for a in range(0, rows, LANES):
            part = slice(a, min(a + LANES, rows))
            scores = mm(keys, q_ref[part, :], ((1,), (1,))) * inv + bias_ref[:, part]
            raised = jnp.exp(scores - jnp.max(scores, axis=0, keepdims=True))
            probs = raised * (1.0 / jnp.sum(raised, axis=0, keepdims=True))
            low = probs.astype(jnp.bfloat16)
            gp = mm(vals, g_ref[part, :], ((1,), (1,)))
            delta = jnp.sum(low.astype(jnp.float32) * gp, axis=0, keepdims=True)
            probs_ref[:, part] = low
            grads_ref[:, part] = (probs * (gp - delta) * inv).astype(jnp.bfloat16)
        gs = grads_ref[...]
        grads = (
            mm(probs_ref[...], g_ref[...], ((1,), (0,))),
            mm(gs, keys, ((0,), (0,))),
            mm(gs, q_ref[...], ((1,), (0,))),
        )
        for n, res in enumerate(grads):
            at = pl.multiple_of(n * width + h * HEAD_DIM, HEAD_DIM)
            result[:, pl.ds(at, HEAD_DIM)] = res.astype(jnp.bfloat16)
        return carry

    lax.fori_loop(0, heads, one_head, 0)
    if count > 1:
        store_blocks(outs, result[...], 0)


def attend(small, blocks, heads):
    count = len(blocks)
    rows = count * blocks[0].shape[0]
    width = heads * HEAD_DIM
    scratch = [
        pltpu.VMEM((rows, rows), jnp.float32),
        pltpu.VMEM((rows, rows), jnp.bfloat16),
        pltpu.VMEM((rows, rows), jnp.bfloat16),
    ]
    if count > 1:
        scratch.append(pltpu.VMEM((rows, 4 * width + LANES), jnp.bfloat16))
        scratch.append(pltpu.VMEM((rows, 3 * width), jnp.bfloat16))
    return call(
        functools.partial(attend_body, heads, count),
        blocks_of(count, rows // count, 3 * width),
        flops=20 * rows * rows * HEAD_DIM * heads,
        moved=14 * rows * heads * HEAD_DIM,
        scratch=scratch,
    )(small, *blocks)


def finish_body(split, *refs):
    va, qa, ka, vb, qb, kb, q_ref, k_ref, qg_ref, kg_ref = refs[:10]
    squares = total_of(refs[10:14])
    inners = total_of(refs[14:18])
    gq_ref, gk_ref, gv_ref = refs[18:]
    spans = (slice(0, split), slice(split, WIDTH_HERE))
    sides = (((qa, qb), q_ref, qg_ref, gq_ref), ((ka, kb), k_ref, kg_ref, gk_ref))
    for n, (pieces, x, gain, out) in enumerate(sides):
        scale = scale_col(squares, n)
        inner = to_col(inners[n : n + 1, :])
        slope = inner / (WIDTH * scale * scale * scale)
        for piece, cols in zip(pieces, spans):
            lifted = piece[...].astype(jnp.float32) * gain[:, cols].astype(jnp.float32)
            result = lifted / scale - x[:, cols].astype(jnp.float32) * slope
            out[:, cols] = result.astype(jnp.bfloat16)
    for piece, cols in zip((va, vb), spans):
        gv_ref[:, cols] = piece[...]


def full_exchange(q_norm, k_norm, values, grad_out, codes, code_row, own_index, small):
    per_source = 2
    slots = 64 * OWNED * per_source
    tokens = jnp.arange(TOK, dtype=jnp.int32)
    code = code_row.reshape(TOK)

    def order_of(c):
        same = (c[..., :, None] == c[..., None, :]) & (tokens[None, :] < tokens[:, None])
        return jnp.sum(same.astype(jnp.int32), axis=-1)

    slot = code * per_source + order_of(code)
    hot = (jnp.arange(slots, dtype=jnp.int32)[:, None] == slot[None, :]).astype(jnp.bfloat16)
    packed = jnp.concatenate([q_norm, k_norm, values, grad_out], axis=1)
    sent = jnp.dot(hot, packed, preferred_element_type=jnp.float32).astype(jnp.bfloat16)
    arrived = lax.all_to_all(sent, "seq", split_axis=0, concat_axis=0, tiled=True)
    slots_here = jnp.arange(OWNED, dtype=jnp.int32) + own_index * OWNED
    held = jnp.sum((codes[:, None, :] == slots_here[None, :, None]).astype(jnp.int32), axis=2)
    live = held[:, :, None] > jnp.arange(per_source, dtype=jnp.int32)[None, None, :]
    local_rows = jnp.where(live, jnp.arange(1, OWNED + 1, dtype=jnp.int32)[None, :, None], 0).reshape(slots)
    bias = bias_of(jnp.broadcast_to(local_rows[:, None], (slots, LANES)), small)
    parts = jnp.transpose(arrived.reshape(slots, 4, HEADS_HERE, HEAD_DIM), (2, 1, 0, 3))
    inv = 1.0 / math.sqrt(HEAD_DIM)

    def one_head(head):
        q, k, v, g = head[0], head[1], head[2], head[3]
        scores = mm(k, q, ((1,), (1,))) * inv + bias
        raised = jnp.exp(scores - jnp.max(scores, axis=0, keepdims=True))
        probs = raised / jnp.sum(raised, axis=0, keepdims=True)
        low = probs.astype(jnp.bfloat16)
        gp = mm(v, g, ((1,), (1,)))
        delta = jnp.sum(low.astype(jnp.float32) * gp, axis=0, keepdims=True)
        gs = (probs * (gp - delta) * inv).astype(jnp.bfloat16)
        return jnp.stack(
            [
                mm(gs, k, ((0,), (0,))).astype(jnp.bfloat16),
                mm(gs, q, ((1,), (0,))).astype(jnp.bfloat16),
                mm(low, g, ((1,), (0,))).astype(jnp.bfloat16),
            ]
        )

    grads = lax.map(one_head, parts)
    back = jnp.transpose(grads, (2, 1, 0, 3)).reshape(slots, 3 * WIDTH_HERE)
    home = lax.all_to_all(back, "seq", split_axis=0, concat_axis=0, tiled=True)
    rows = lax.dot_general(
        hot, home, (((0,), (0,)), ((), ())), preferred_element_type=jnp.float32
    ).astype(jnp.bfloat16)
    return tuple(rows[:, n * WIDTH_HERE : (n + 1) * WIDTH_HERE] for n in range(3))


def on_device(
    query_raw, key_raw, values, grad_out, query_gain, key_gain, cluster_of, pair_mask, cluster_owner
):
    own_index = lax.axis_index("seq").astype(jnp.int32)
    z_here = own_index // NR
    q_gain = query_gain.reshape(1, WIDTH_HERE)
    k_gain = key_gain.reshape(1, WIDTH_HERE)
    table_row, code_row, dest_a, dest_b = prep(cluster_of, cluster_owner, z_here)
    row_sums = jax.ShapeDtypeStruct((8, TOK), jnp.float32)
    norms = over_head(call(squares_body, row_sums)(query_raw, key_raw))
    raw_args = (code_row, values, grad_out, query_raw, key_raw, q_gain, k_gain, *norms)

    heads_b = HEADS_HERE - HEADS_A
    a_packed = pack(0, HEADS_A, NZ, (dest_a, *raw_args))
    a_sent = z_exchange(a_packed, 1)
    (b_packed,) = pack(HEADS_A, HEADS_HERE, 1, (dest_b, *raw_args))
    b_middle = y_exchange(b_packed)
    b_blocks, b_table = spread("z", (b_middle,), NZ, Z_CAP, z_here)
    code_late, b_table = lax.optimization_barrier((code_row, b_table))
    codes = lax.all_to_all(
        jnp.broadcast_to(code_late, (NZ * NR, TOK)), "seq", split_axis=0, concat_axis=0, tiled=True
    )
    small = small_mask(table_row, pair_mask, own_index)
    overflow = overflow_count(codes)

    b_arrived = z_exchange(b_blocks, 1)
    (a_rows,), a_table = spread("y", a_sent, 1, Y_CAP, z_here)
    a_arrived = y_exchange(a_rows)
    b_grads = attend(small, b_arrived, heads_b)
    b_return = z_exchange(b_grads, -1)
    (a_grads,) = attend(small, (a_arrived,), HEADS_A)
    a_back = y_exchange(a_grads)
    a_blocks = gather(a_table, (a_back,), NZ, Y_CAP)
    a_return = z_exchange(a_blocks, -1)
    (b_rows,) = gather(b_table, b_return, 1, Z_CAP)
    b_home = y_exchange(b_rows)
    sides = (query_raw, key_raw, q_gain, k_gain)
    piece_a = unpack(0, HEADS_A, dest_a, sides, a_return)
    piece_b = unpack(HEADS_A, HEADS_HERE, dest_b, sides, (b_home,))
    inner = piece_a[3] + piece_b[3]

    split = HEADS_A * HEAD_DIM

    given = (*norms, query_raw, key_raw, values, grad_out, q_gain, k_gain, codes, code_row, small)

    def slow(state):
        trip, inputs = lax.optimization_barrier((state[0], given))
        return redo(trip, *inputs)

    def redo(trip, n0, n1, n2, n3, query_raw, key_raw, values, grad_out, q_gain, k_gain, codes, code_row, small):
        squares = (n0 + n1) + (n2 + n3)
        scales = jnp.sqrt(squares / WIDTH + EPSILON)
        q_norm = normed(query_raw, q_gain, scales[0][:, None])
        k_norm = normed(key_raw, k_gain, scales[1][:, None])
        home_q, home_k, home_v = full_exchange(
            q_norm, k_norm, values, grad_out, codes, code_row, own_index, small
        )
        parts = [
            jnp.sum(h.astype(jnp.float32) * g.astype(jnp.float32) * x.astype(jnp.float32), axis=1)
            for h, g, x in ((home_q, q_gain, query_raw), (home_k, k_gain, key_raw))
        ]
        rows = jnp.concatenate([jnp.stack(parts), jnp.zeros((6, TOK), jnp.float32)])
        homes = (home_v, home_q, home_k)
        return (
            trip + 1,
            tuple(h[:, :split] for h in homes),
            tuple(h[:, split:] for h in homes),
            rows,
        )

    _, home_a, home_b, inner = lax.while_loop(
        lambda state: state[0] < overflow, slow, (jnp.int32(0), piece_a[:3], piece_b[:3], inner)
    )
    inners = over_head(inner)
    out = jax.ShapeDtypeStruct((TOK, WIDTH_HERE), jnp.bfloat16)
    return call(functools.partial(finish_body, split), (out,) * 3)(
        *home_a, *home_b, *sides, *norms, *inners
    )


def solution(mesh):
    return jax.shard_map(
        on_device,
        mesh=mesh,
        in_specs=(
            P("seq", "head"),
            P("seq", "head"),
            P("seq", "head"),
            P("seq", "head"),
            P("head"),
            P("head"),
            P("seq"),
            P(),
            P(),
        ),
        out_specs=(P("seq", "head"), P("seq", "head"), P("seq", "head")),
        check_vma=False,
    )
```

```python
import functools
import math

import jax
import jax.numpy as jnp
from jax import lax
from jax.experimental import pallas as pl
from jax.experimental.pallas import tpu as pltpu
from jax.sharding import PartitionSpec as P


WIDTH = 5120
HEAD_DIM = 128
EPSILON = 1e-06
NEGATIVE = -1e30

TOK = 256
NZ = 8
NR = 8
OWNED = 4
SRC_CAP = 48
Y_CAP = 56
Z_CAP = 56
SRC_ROWS = NZ * SRC_CAP
WIDTH_HERE = 1280
HEADS_HERE = 10
GROUPS_A = ((0, 5),)
GROUPS_B = ((5, 8), (8, 10))
SPLIT = 5 * HEAD_DIM
LANES = 128


Y_GROUPS = [[NR * z + r for r in range(NR)] for z in range(NZ)]


def z_perm(shift):
    return [(s, ((s // NR + shift) % NZ) * NR + s % NR) for s in range(NZ * NR)]


def head_perm(shift):
    return [(s, (s + shift) % 4) for s in range(4)]


def call(body, out_shape, flops=0, moved=0, scratch=()):
    return pl.pallas_call(
        body,
        out_shape=out_shape,
        scratch_shapes=scratch,
        cost_estimate=pl.CostEstimate(flops=flops, bytes_accessed=moved, transcendentals=0),
        compiler_params=pltpu.CompilerParams(vmem_limit_bytes=20 * 1024 * 1024),
    )


def iota(shape, dim):
    return lax.broadcasted_iota(jnp.int32, shape, dim)


def to_col(row):
    n = row.shape[1]
    eye = iota((n, n), 0) == iota((n, n), 1)
    return jnp.sum(jnp.where(eye, jnp.broadcast_to(row, (n, n)), jnp.zeros((), row.dtype)), axis=1, keepdims=True)


def to_row(col):
    n = col.shape[0]
    eye = iota((n, n), 0) == iota((n, n), 1)
    return jnp.sum(jnp.where(eye, jnp.broadcast_to(col, (n, n)), jnp.zeros((), col.dtype)), axis=0, keepdims=True)


def mm(a, b, dims):
    return lax.dot_general(a, b, (dims, ((), ())), preferred_element_type=jnp.float32)


def prep_body(cluster_ref, owner_ref, z_ref, table_ref, code_ref, dest_a_ref, dest_b_ref):
    square = (TOK, TOK)
    owner_row = owner_ref[...]
    owner_col = to_col(owner_row)
    earlier = iota(square, 0) < iota(square, 1)
    one, zero = jnp.int32(1), jnp.int32(0)
    local_row = jnp.sum(
        jnp.where((owner_col == owner_row) & earlier, one, zero), axis=0, keepdims=True
    )
    table_row = owner_row * OWNED + local_row
    table_ref[...] = table_row
    table_col = to_col(table_row)
    code_row = jnp.sum(
        jnp.where(iota(square, 0) == cluster_ref[...], table_col, zero), axis=0, keepdims=True
    )
    code_ref[...] = code_row
    for key_row, out_ref in (
        (((code_row >> 5) - z_ref[0] + NZ) & (NZ - 1), dest_a_ref),
        ((code_row >> 2) & (NR - 1), dest_b_ref),
    ):
        key_col = to_col(key_row)
        rank_row = jnp.sum(
            jnp.where((key_col == key_row) & earlier, one, zero), axis=0, keepdims=True
        )
        out_ref[...] = jnp.where(rank_row < SRC_CAP, key_row * SRC_CAP + rank_row, -1)


VMEM_SPEC = pl.BlockSpec(memory_space=pltpu.VMEM)
SMEM_SPEC = pl.BlockSpec(memory_space=pltpu.SMEM)


def prep(cluster_of, cluster_owner, z_here):
    row = jax.ShapeDtypeStruct((1, TOK), jnp.int32)
    return pl.pallas_call(
        prep_body,
        out_shape=(row,) * 4,
        in_specs=[VMEM_SPEC, VMEM_SPEC, SMEM_SPEC],
        out_specs=(VMEM_SPEC,) * 4,
        name="prep",
    )(cluster_of.reshape(1, TOK), cluster_owner.reshape(1, TOK), z_here.reshape(1))


def mask_body(table_ref, mask_ref, own_ref, out_ref):
    slots = iota((LANES, TOK), 0)
    chosen = (table_ref[...] == own_ref[0] * OWNED + slots) & (slots < OWNED)
    chosen = jnp.where(chosen, 1.0, 0.0).astype(jnp.bfloat16)
    pairs = mask_ref[...].astype(jnp.float32).astype(jnp.bfloat16)
    rows = mm(chosen, pairs, ((1,), (0,))).astype(jnp.bfloat16)
    out_ref[...] = mm(rows, chosen, ((1,), (1,))).astype(jnp.bfloat16)


def small_mask(table_row, pair_mask, own_index):
    return pl.pallas_call(
        mask_body,
        out_shape=jax.ShapeDtypeStruct((LANES, LANES), jnp.bfloat16),
        in_specs=[VMEM_SPEC, VMEM_SPEC, SMEM_SPEC],
        out_specs=VMEM_SPEC,
        name="mask",
    )(table_row, pair_mask, own_index.reshape(1))


def bias_of(code, small):
    local = jnp.where(code > 0, (code - 1) & (OWNED - 1), -1)
    hot = jnp.where(local == iota(local.shape, 1), 1.0, 0.0).astype(jnp.bfloat16)
    reach = mm(hot, small, ((1,), (1,))).astype(jnp.bfloat16)
    return jnp.where(mm(reach, hot, ((1,), (1,))) > 0.5, 0.0, NEGATIVE)


def overflow_count(codes):
    hit = (codes >> 2)[:, None, :] == jnp.arange(NZ * NR, dtype=jnp.int32)[None, :, None]
    count = jnp.sum(hit.astype(jnp.int32), axis=2).reshape(NZ, NR, NZ, NR)
    most = [
        jnp.max(jnp.sum(count, axis=dim)) - cap
        for dim, cap in ((3, SRC_CAP), (2, SRC_CAP), (1, Z_CAP), (0, Y_CAP))
    ]
    return (functools.reduce(jnp.maximum, most) > 0).astype(jnp.int32)


def squares_body(q_ref, k_ref, out_ref):
    q = q_ref[...].astype(jnp.float32)
    k = k_ref[...].astype(jnp.float32)
    out_ref[0:1, :] = to_row(jnp.sum(q * q, axis=1, keepdims=True))
    out_ref[1:2, :] = to_row(jnp.sum(k * k, axis=1, keepdims=True))
    out_ref[2:8, :] = jnp.zeros((6, TOK), jnp.float32)


def over_head(part):
    return [part] + [lax.ppermute(part, "head", head_perm(d)) for d in (1, 2, 3)]


def total_of(refs):
    return (refs[0][...] + refs[1][...]) + (refs[2][...] + refs[3][...])


def scale_col(total, which):
    return jnp.sqrt(to_col(total[which : which + 1, :]) / WIDTH + EPSILON)


def place_rows(dest_row):
    return jnp.where(iota((SRC_ROWS, TOK), 0) == dest_row, 1.0, 0.0).astype(jnp.bfloat16)


def store_blocks(outs, packed, start):
    width = packed.shape[1]
    cap = packed.shape[0] // len(outs)
    for d, out in enumerate(outs):
        out[:, start : start + width] = packed[d * cap : (d + 1) * cap, :]


def normed(raw, gain, scale):
    return (raw.astype(jnp.float32) * gain.astype(jnp.float32) / scale).astype(jnp.bfloat16)


def widths_of(groups):
    return [(hi - lo) * HEAD_DIM for lo, hi in groups]


def pack_body(groups, dest_ref, code_ref, v_ref, g_ref, q_ref, k_ref, qg_ref, kg_ref, *refs):
    total = total_of(refs[:4])
    outs = refs[4:]
    hot = place_rows(dest_ref[...])
    at = 0

    def put(part):
        store_blocks(outs, mm(hot, part, ((1,), (0,))).astype(jnp.bfloat16), at)
        return at + part.shape[1]

    code = jnp.broadcast_to(to_col(code_ref[...]) + 1, (TOK, LANES))
    at = put(code.astype(jnp.float32).astype(jnp.bfloat16))
    sides = [
        (ref, gain, scale_col(total, which))
        for which, (ref, gain) in enumerate(((q_ref, qg_ref), (k_ref, kg_ref)))
    ]
    for lo, hi in groups:
        cols = slice(lo * HEAD_DIM, hi * HEAD_DIM)
        at = put(v_ref[:, cols])
        at = put(g_ref[:, cols])
        for ref, gain, scale in sides:
            at = put(normed(ref[:, cols], gain[:, cols], scale))


def blocks_of(count, rows, width):
    return (jax.ShapeDtypeStruct((rows, width), jnp.bfloat16),) * count


def pack(groups, count, args):
    width = sum(widths_of(groups)) * 4 + LANES
    return call(
        functools.partial(pack_body, groups),
        blocks_of(count, SRC_ROWS // count, width),
        flops=2 * SRC_ROWS * TOK * width,
        moved=4 * SRC_ROWS * width,
    )(*args)


def z_exchange(blocks, sign):
    return [blocks[0]] + [
        lax.ppermute(blocks[d], "seq", z_perm(sign * d)) for d in range(1, NZ)
    ]


def y_exchange(rows):
    return lax.all_to_all(
        rows, "seq", split_axis=0, concat_axis=0, axis_index_groups=Y_GROUPS, tiled=True
    )


def stacked(blocks, cols):
    if len(blocks) == 1:
        return blocks[0][:, cols]
    return jnp.concatenate([b[:, cols] for b in blocks], axis=0)


def steps_of(width):
    return [slice(a, min(a + 512, width)) for a in range(0, width, 512)]


def spread_body(mode, count_in, cap, z_ref, *refs):
    blocks, outs, table_ref = refs[:count_in], refs[count_in:-1], refs[-1]
    code = stacked(blocks, slice(0, LANES)).astype(jnp.float32).astype(jnp.int32)[:, 0:1]
    if mode == "y":
        key = ((code - 1) >> 2) & (NR - 1)
    else:
        key = (((code - 1) >> 5) - z_ref[0] + NZ) & (NZ - 1)
    key_col = jnp.where(code > 0, key, -1)
    key_row = to_row(key_col)
    square = (SRC_ROWS, SRC_ROWS)
    before = (key_col == key_row) & (iota(square, 0) < iota(square, 1))
    rank_row = jnp.sum(jnp.where(before, jnp.int32(1), jnp.int32(0)), axis=0, keepdims=True)
    dest = jnp.where((key_row >= 0) & (rank_row < cap), key_row * cap + rank_row, -1)
    table_ref[...] = dest
    hot = jnp.where(iota((NZ * cap, SRC_ROWS), 0) == dest, 1.0, 0.0).astype(jnp.bfloat16)
    per = 1 if mode == "y" else NZ
    start = 0
    for n in range(0, len(outs), per):
        group = outs[n : n + per]
        width = group[0].shape[1]
        for cols in steps_of(width):
            rows = stacked(blocks, slice(start + cols.start, start + cols.stop))
            store_blocks(group, mm(hot, rows, ((1,), (0,))).astype(jnp.bfloat16), cols.start)
        start += width


def spread(mode, blocks, widths, cap, z_here):
    per = 1 if mode == "y" else NZ
    shapes = sum((blocks_of(per, NZ * cap // per, width) for width in widths), ())
    outs = pl.pallas_call(
        functools.partial(spread_body, mode, len(blocks), cap),
        out_shape=shapes + (jax.ShapeDtypeStruct((1, SRC_ROWS), jnp.int32),),
        in_specs=[SMEM_SPEC] + [VMEM_SPEC] * len(blocks),
        out_specs=(VMEM_SPEC,) * (len(shapes) + 1),
        cost_estimate=pl.CostEstimate(
            flops=2 * NZ * cap * SRC_ROWS * sum(widths), bytes_accessed=0, transcendentals=0
        ),
        compiler_params=pltpu.CompilerParams(vmem_limit_bytes=20 * 1024 * 1024),
    )(z_here.reshape(1), *blocks)
    return [outs[n * per : (n + 1) * per] for n in range(len(widths))], outs[-1]


def gather_body(counts, cap, table_ref, *refs):
    outs = refs[sum(counts) :]
    hot = jnp.where(iota((NZ * cap, SRC_ROWS), 0) == table_ref[...], 1.0, 0.0).astype(jnp.bfloat16)
    start = first = 0
    for count in counts:
        blocks = refs[first : first + count]
        first += count
        width = blocks[0].shape[1]
        for cols in steps_of(width):
            packed = mm(hot, stacked(blocks, cols), ((0,), (0,))).astype(jnp.bfloat16)
            store_blocks(outs, packed, start + cols.start)
        start += width


def gather(table, groups, count_out, cap):
    width = sum(blocks[0].shape[1] for blocks in groups)
    return call(
        functools.partial(gather_body, [len(blocks) for blocks in groups], cap),
        blocks_of(count_out, SRC_ROWS // count_out, width),
        flops=2 * NZ * cap * SRC_ROWS * width,
        moved=4 * NZ * cap * width,
    )(table, *[block for blocks in groups for block in blocks])


def inner_row(grad, raw, gain):
    lifted = grad.astype(jnp.float32) * gain.astype(jnp.float32)
    return to_row(jnp.sum(lifted * raw.astype(jnp.float32), axis=1, keepdims=True))


def unpack_body(groups, dest_ref, q_ref, k_ref, qg_ref, kg_ref, *refs):
    blocks, outs, inner_ref = refs[:-4], refs[-4:-1], refs[-1]
    hot = place_rows(dest_ref[...])
    sides = (None, (q_ref, qg_ref), (k_ref, kg_ref))
    inner_ref[...] = jnp.zeros((8, TOK), jnp.float32)
    at = 0
    for lo, hi in groups:
        width = (hi - lo) * HEAD_DIM
        cols = slice(lo * HEAD_DIM, hi * HEAD_DIM)
        base = (lo - groups[0][0]) * HEAD_DIM
        for n, (out, side) in enumerate(zip(outs, sides)):
            grad = mm(hot, stacked(blocks, slice(at, at + width)), ((0,), (0,))).astype(jnp.bfloat16)
            at += width
            out[:, base : base + width] = grad
            if side is not None:
                inner_ref[n - 1 : n, :] += inner_row(grad, side[0][:, cols], side[1][:, cols])


def unpack(groups, dest, sides, blocks):
    width = sum(widths_of(groups))
    return call(
        functools.partial(unpack_body, groups),
        blocks_of(3, TOK, width) + (jax.ShapeDtypeStruct((8, TOK), jnp.float32),),
        flops=2 * SRC_ROWS * TOK * width * 3,
        moved=4 * SRC_ROWS * width * 3,
    )(dest, *sides, *blocks)


def attend_body(heads, count, first, mask_ref, *refs):
    if not first:
        refs = refs[1 : 1 + 2 * count] + refs[:1] + refs[1 + 2 * count :]
    blocks, outs = refs[:count], refs[count : 2 * count]
    scratch = list(refs[2 * count :])
    code_ref = scratch.pop(0)
    bias_ref, probs_ref, grads_ref = scratch[:3]
    rows, width = bias_ref.shape[0], heads * HEAD_DIM
    base = LANES if first else 0
    if count == 1:
        data, result = blocks[0], outs[0]
    else:
        data, result = scratch[3:]
        cap = rows // count
        for d, block in enumerate(blocks):
            data[d * cap : (d + 1) * cap, :] = block[...]
    inv = 1.0 / math.sqrt(HEAD_DIM)
    if first:
        code_ref[...] = data[:, :LANES]
    bias_ref[...] = bias_of(code_ref[...].astype(jnp.float32).astype(jnp.int32), mask_ref[...])

    def one_head(h, carry):
        v_ref, g_ref, q_ref, k_ref = (
            data.at[:, pl.ds(pl.multiple_of(base + n * width + h * HEAD_DIM, HEAD_DIM), HEAD_DIM)]
            for n in range(4)
        )
        keys = k_ref[...]
        vals = v_ref[...]
        for a in range(0, rows, LANES):
            part = slice(a, min(a + LANES, rows))
            scores = mm(keys, q_ref[part, :], ((1,), (1,))) * inv + bias_ref[:, part]
            raised = jnp.exp(scores - jnp.max(scores, axis=0, keepdims=True))
            probs = raised * (1.0 / jnp.sum(raised, axis=0, keepdims=True))
            low = probs.astype(jnp.bfloat16)
            gp = mm(vals, g_ref[part, :], ((1,), (1,)))
            delta = jnp.sum(low.astype(jnp.float32) * gp, axis=0, keepdims=True)
            probs_ref[:, part] = low
            grads_ref[:, part] = (probs * (gp - delta) * inv).astype(jnp.bfloat16)
        gs = grads_ref[...]
        grads = (
            mm(probs_ref[...], g_ref[...], ((1,), (0,))),
            mm(gs, keys, ((0,), (0,))),
            mm(gs, q_ref[...], ((1,), (0,))),
        )
        for n, res in enumerate(grads):
            at = pl.multiple_of(n * width + h * HEAD_DIM, HEAD_DIM)
            result[:, pl.ds(at, HEAD_DIM)] = res.astype(jnp.bfloat16)
        return carry

    lax.fori_loop(0, heads, one_head, 0)
    if count > 1:
        store_blocks(outs, result[...], 0)


def attend(mask, blocks, heads, code=None):
    first = code is None
    count = len(blocks)
    rows = count * blocks[0].shape[0]
    width = heads * HEAD_DIM
    square = (rows, rows)
    scratch = [pltpu.VMEM(square, kind) for kind in (jnp.float32, jnp.bfloat16, jnp.bfloat16)]
    if count > 1:
        scratch.append(pltpu.VMEM((rows, blocks[0].shape[1]), jnp.bfloat16))
        scratch.append(pltpu.VMEM((rows, 3 * width), jnp.bfloat16))
    shapes = blocks_of(count, rows // count, 3 * width)
    if first:
        shapes += blocks_of(1, rows, LANES)
    outs = call(
        functools.partial(attend_body, heads, count, first),
        shapes,
        flops=20 * rows * rows * HEAD_DIM * heads,
        moved=14 * rows * heads * HEAD_DIM,
        scratch=scratch,
    )(mask, *(() if first else (code,)), *blocks)
    return outs[:count], outs[count:]


def finish_body(*refs):
    va, qa, ka, vb, qb, kb, q_ref, k_ref, qg_ref, kg_ref = refs[:10]
    squares = total_of(refs[10:14])
    inners = total_of(refs[14:18])
    gq_ref, gk_ref, gv_ref = refs[18:]
    spans = (slice(0, SPLIT), slice(SPLIT, WIDTH_HERE))
    sides = (((qa, qb), q_ref, qg_ref, gq_ref), ((ka, kb), k_ref, kg_ref, gk_ref))
    for n, (pieces, x, gain, out) in enumerate(sides):
        scale = scale_col(squares, n)
        inner = to_col(inners[n : n + 1, :])
        slope = inner / (WIDTH * scale * scale * scale)
        for piece, cols in zip(pieces, spans):
            lifted = piece[...].astype(jnp.float32) * gain[:, cols].astype(jnp.float32)
            result = lifted / scale - x[:, cols].astype(jnp.float32) * slope
            out[:, cols] = result.astype(jnp.bfloat16)
    for piece, cols in zip((va, vb), spans):
        gv_ref[:, cols] = piece[...]


FULL = 64 * OWNED * 2
TILE = pl.BlockSpec((TOK, HEAD_DIM), lambda n: (0, n))


def fixed(shape):
    return pl.BlockSpec(shape, lambda n: (0, 0))


def stack_tile(count, rows):
    return pl.BlockSpec((count, rows, HEAD_DIM), lambda n: (0, 0, n))


def full_slots(slot_row):
    return jnp.where(iota((FULL, TOK), 0) == slot_row, 1.0, 0.0).astype(jnp.bfloat16)


def full_pack_body(slot_ref, *refs):
    hot = full_slots(slot_ref[...])
    for n, ref in enumerate(refs[:4]):
        refs[4][n] = mm(hot, ref[...], ((1,), (0,))).astype(jnp.bfloat16)


def full_unpack_body(slot_ref, in_ref, out_ref):
    hot = full_slots(slot_ref[...])
    for n in range(3):
        out_ref[n] = mm(hot, in_ref[n], ((0,), (0,))).astype(jnp.bfloat16)


def full_attend_body(mask_ref, code_ref, in_ref, out_ref):
    inv = 1.0 / math.sqrt(HEAD_DIM)
    q, k, v, g = (in_ref[n] for n in range(4))
    scores = mm(k, q, ((1,), (1,))) * inv + bias_of(code_ref[...], mask_ref[...])
    raised = jnp.exp(scores - jnp.max(scores, axis=0, keepdims=True))
    probs = raised / jnp.sum(raised, axis=0, keepdims=True)
    low = probs.astype(jnp.bfloat16)
    gp = mm(v, g, ((1,), (1,)))
    delta = jnp.sum(low.astype(jnp.float32) * gp, axis=0, keepdims=True)
    gs = (probs * (gp - delta) * inv).astype(jnp.bfloat16)
    out_ref[0] = mm(gs, k, ((0,), (0,))).astype(jnp.bfloat16)
    out_ref[1] = mm(gs, q, ((1,), (0,))).astype(jnp.bfloat16)
    out_ref[2] = mm(low, g, ((1,), (0,))).astype(jnp.bfloat16)


def by_head(body, ins, specs, count, rows):
    return pl.pallas_call(
        body,
        grid=(HEADS_HERE,),
        out_shape=jax.ShapeDtypeStruct((count, rows, WIDTH_HERE), jnp.bfloat16),
        in_specs=specs,
        out_specs=stack_tile(count, rows),
        compiler_params=pltpu.CompilerParams(vmem_limit_bytes=20 * 1024 * 1024),
    )(*ins)


def full_exchange(q_norm, k_norm, values, grad_out, codes, code_row, own_index, small):
    square = (TOK, TOK)
    code_col = code_row.reshape(TOK, 1)
    same = (code_col == code_row) & (iota(square, 0) < iota(square, 1))
    slot_row = code_row * 2 + jnp.sum(same.astype(jnp.int32), axis=0, keepdims=True)
    slots_here = jnp.arange(OWNED, dtype=jnp.int32) + own_index * OWNED
    held = jnp.sum((codes[:, None, :] == slots_here[None, :, None]).astype(jnp.int32), axis=2)
    live = held[:, :, None] > jnp.arange(2, dtype=jnp.int32)[None, None, :]
    rows = jnp.where(live, jnp.arange(1, OWNED + 1, dtype=jnp.int32)[None, :, None], 0)
    code = jnp.broadcast_to(rows.reshape(FULL, 1), (FULL, LANES))

    def swap(array):
        return lax.all_to_all(array, "seq", split_axis=0, concat_axis=0, tiled=True)

    row = fixed((1, TOK))
    raws = (q_norm, k_norm, values, grad_out)
    sent = by_head(full_pack_body, (slot_row, *raws), [row] + [TILE] * 4, 4, FULL)
    arrived = lax.map(swap, sent)
    grads = by_head(
        full_attend_body,
        (small, code, arrived),
        [fixed((LANES, LANES)), fixed((FULL, LANES)), stack_tile(4, FULL)],
        3,
        FULL,
    )
    home = lax.map(swap, grads)
    rows = by_head(full_unpack_body, (slot_row, home), [row, stack_tile(3, FULL)], 3, TOK)
    return rows[0], rows[1], rows[2]


def on_device(
    query_raw, key_raw, values, grad_out, query_gain, key_gain, cluster_of, pair_mask, cluster_owner
):
    own_index = lax.axis_index("seq").astype(jnp.int32)
    z_here = own_index // NR
    q_gain = query_gain.reshape(1, WIDTH_HERE)
    k_gain = key_gain.reshape(1, WIDTH_HERE)
    table_row, code_row, dest_a, dest_b = prep(cluster_of, cluster_owner, z_here)
    row_sums = jax.ShapeDtypeStruct((8, TOK), jnp.float32)
    norms = over_head(call(squares_body, row_sums)(query_raw, key_raw))
    raw_args = (code_row, values, grad_out, query_raw, key_raw, q_gain, k_gain, *norms)

    a_packed = pack(GROUPS_A, NZ, (dest_a, *raw_args))
    a_sent = z_exchange(a_packed, 1)
    (b_packed,) = pack(GROUPS_B, 1, (dest_b, *raw_args))
    b_middle = y_exchange(b_packed)
    small = small_mask(table_row, pair_mask, own_index)

    b_wide, c_wide = widths_of(GROUPS_B)
    (b_blocks, c_blocks), b_table = spread(
        "z", (b_middle,), (LANES + 4 * b_wide, 4 * c_wide), Z_CAP, z_here
    )
    b_arrived = z_exchange(b_blocks, 1)
    c_arrived = z_exchange(c_blocks, 1)
    ((a_rows,),), a_table = spread(
        "y", a_sent, (LANES + 4 * SPLIT,), Y_CAP, z_here
    )
    a_arrived = y_exchange(a_rows)
    b_grads, (b_code,) = attend(small, b_arrived, b_wide // HEAD_DIM)
    b_return = z_exchange(b_grads, -1)
    (a_grads,), _ = attend(small, (a_arrived,), SPLIT // HEAD_DIM)
    a_back = y_exchange(a_grads)
    c_grads, _ = attend(small, c_arrived, c_wide // HEAD_DIM, b_code)
    c_return = z_exchange(c_grads, -1)
    a_blocks = gather(a_table, ((a_back,),), NZ, Y_CAP)
    a_return = z_exchange(a_blocks, -1)
    code_late, _ = lax.optimization_barrier((code_row, a_blocks[0]))
    codes = lax.all_to_all(
        jnp.broadcast_to(code_late, (NZ * NR, TOK)), "seq", split_axis=0, concat_axis=0, tiled=True
    )
    (b_rows,) = gather(b_table, (b_return, c_return), 1, Z_CAP)
    b_home = y_exchange(b_rows)
    overflow = overflow_count(codes)
    sides = (query_raw, key_raw, q_gain, k_gain)
    piece_b = unpack(GROUPS_B, dest_b, sides, (b_home,))
    piece_a = unpack(GROUPS_A, dest_a, sides, a_return)
    inner = piece_a[3] + piece_b[3]

    given = (*norms, query_raw, key_raw, values, grad_out, q_gain, k_gain, codes, code_row, small)

    def slow(state):
        trip, inputs = lax.optimization_barrier((state[0], given))
        return redo(trip, *inputs)

    def redo(trip, n0, n1, n2, n3, query_raw, key_raw, values, grad_out, q_gain, k_gain, codes, code_row, small):
        squares = (n0 + n1) + (n2 + n3)
        scales = jnp.sqrt(squares / WIDTH + EPSILON)
        q_norm = normed(query_raw, q_gain, scales[0][:, None])
        k_norm = normed(key_raw, k_gain, scales[1][:, None])
        home_q, home_k, home_v = full_exchange(
            q_norm, k_norm, values, grad_out, codes, code_row, own_index, small
        )
        parts = [
            jnp.sum(h.astype(jnp.float32) * g.astype(jnp.float32) * x.astype(jnp.float32), axis=1)
            for h, g, x in ((home_q, q_gain, query_raw), (home_k, k_gain, key_raw))
        ]
        rows = jnp.concatenate([jnp.stack(parts), jnp.zeros((6, TOK), jnp.float32)])
        homes = (home_v, home_q, home_k)
        return (
            trip + 1,
            tuple(h[:, :SPLIT] for h in homes),
            tuple(h[:, SPLIT:] for h in homes),
            rows,
        )

    _, home_a, home_b, inner = lax.while_loop(
        lambda state: state[0] < overflow, slow, (jnp.int32(0), piece_a[:3], piece_b[:3], inner)
    )
    inners = over_head(inner)
    out = jax.ShapeDtypeStruct((TOK, WIDTH_HERE), jnp.bfloat16)
    return call(finish_body, (out,) * 3)(
        *home_a, *home_b, *sides, *norms, *inners
    )


def solution(mesh):
    return jax.shard_map(
        on_device,
        mesh=mesh,
        in_specs=(
            P("seq", "head"),
            P("seq", "head"),
            P("seq", "head"),
            P("seq", "head"),
            P("head"),
            P("head"),
            P("seq"),
            P(),
            P(),
        ),
        out_specs=(P("seq", "head"), P("seq", "head"), P("seq", "head")),
        check_vma=False,
    )
```

```python
import functools
import math

import jax
import jax.numpy as jnp
from jax import lax
from jax.experimental import pallas as pl
from jax.experimental.pallas import tpu as pltpu
from jax.sharding import PartitionSpec as P


WIDTH = 5120
HEAD_DIM = 128
EPSILON = 1e-06
NEGATIVE = -1e30

TOK = 256
NZ = 8
NR = 8
OWNED = 4
SRC_CAP = 48
Y_CAP = 56
Z_CAP = 56
SRC_ROWS = NZ * SRC_CAP
WIDTH_HERE = 1280
HEADS_HERE = 10
GROUPS_A = ((0, 5),)
GROUPS_B = ((5, 10),)
SPLIT = 5 * HEAD_DIM
LANES = 128


Y_GROUPS = [[NR * z + r for r in range(NR)] for z in range(NZ)]


def z_perm(shift):
    return [(s, ((s // NR + shift) % NZ) * NR + s % NR) for s in range(NZ * NR)]


def head_perm(shift):
    return [(s, (s + shift) % 4) for s in range(4)]


def call(body, out_shape, flops=0, moved=0, scratch=()):
    return pl.pallas_call(
        body,
        out_shape=out_shape,
        scratch_shapes=scratch,
        cost_estimate=pl.CostEstimate(flops=flops, bytes_accessed=moved, transcendentals=0),
        compiler_params=pltpu.CompilerParams(vmem_limit_bytes=20 * 1024 * 1024),
    )


def iota(shape, dim):
    return lax.broadcasted_iota(jnp.int32, shape, dim)


def to_col(row):
    n = row.shape[1]
    eye = iota((n, n), 0) == iota((n, n), 1)
    return jnp.sum(jnp.where(eye, jnp.broadcast_to(row, (n, n)), jnp.zeros((), row.dtype)), axis=1, keepdims=True)


def to_row(col):
    n = col.shape[0]
    eye = iota((n, n), 0) == iota((n, n), 1)
    return jnp.sum(jnp.where(eye, jnp.broadcast_to(col, (n, n)), jnp.zeros((), col.dtype)), axis=0, keepdims=True)


def mm(a, b, dims):
    return lax.dot_general(a, b, (dims, ((), ())), preferred_element_type=jnp.float32)


def prep_body(cluster_ref, owner_ref, z_ref, table_ref, code_ref, dest_a_ref, dest_b_ref, flag_ref):
    square = (TOK, TOK)
    owner_row = owner_ref[...]
    owner_col = to_col(owner_row)
    earlier = iota(square, 0) < iota(square, 1)
    one, zero = jnp.int32(1), jnp.int32(0)
    local_row = jnp.sum(
        jnp.where((owner_col == owner_row) & earlier, one, zero), axis=0, keepdims=True
    )
    table_row = owner_row * OWNED + local_row
    table_ref[...] = table_row
    table_col = to_col(table_row)
    code_row = jnp.sum(
        jnp.where(iota(square, 0) == cluster_ref[...], table_col, zero), axis=0, keepdims=True
    )
    code_ref[...] = code_row
    ranks = []
    for key_row, out_ref in (
        (((code_row >> 5) - z_ref[0] + NZ) & (NZ - 1), dest_a_ref),
        ((code_row >> 2) & (NR - 1), dest_b_ref),
    ):
        key_col = to_col(key_row)
        rank_row = jnp.sum(
            jnp.where((key_col == key_row) & earlier, one, zero), axis=0, keepdims=True
        )
        out_ref[...] = jnp.where(rank_row < SRC_CAP, key_row * SRC_CAP + rank_row, -1)
        ranks.append(rank_row)
    most = jnp.max(jnp.maximum(ranks[0], ranks[1]), axis=1, keepdims=True)
    flag_ref[...] = jnp.broadcast_to(jnp.where(most < SRC_CAP, 0.0, 1.0), (1, LANES))


FLAG = jax.ShapeDtypeStruct((1, LANES), jnp.float32)
VMEM_SPEC = pl.BlockSpec(memory_space=pltpu.VMEM)
SMEM_SPEC = pl.BlockSpec(memory_space=pltpu.SMEM)


def prep(cluster_of, cluster_owner, z_here):
    row = jax.ShapeDtypeStruct((1, TOK), jnp.int32)
    return pl.pallas_call(
        prep_body,
        out_shape=(row,) * 4 + (FLAG,),
        in_specs=[VMEM_SPEC, VMEM_SPEC, SMEM_SPEC],
        out_specs=(VMEM_SPEC,) * 5,
        name="prep",
    )(cluster_of.reshape(1, TOK), cluster_owner.reshape(1, TOK), z_here.reshape(1))


def mask_body(table_ref, mask_ref, own_ref, out_ref):
    slots = iota((LANES, TOK), 0)
    chosen = (table_ref[...] == own_ref[0] * OWNED + slots) & (slots < OWNED)
    chosen = jnp.where(chosen, 1.0, 0.0).astype(jnp.bfloat16)
    pairs = mask_ref[...].astype(jnp.float32).astype(jnp.bfloat16)
    rows = mm(chosen, pairs, ((1,), (0,))).astype(jnp.bfloat16)
    out_ref[...] = mm(rows, chosen, ((1,), (1,))).astype(jnp.bfloat16)


def small_mask(table_row, pair_mask, own_index):
    return pl.pallas_call(
        mask_body,
        out_shape=jax.ShapeDtypeStruct((LANES, LANES), jnp.bfloat16),
        in_specs=[VMEM_SPEC, VMEM_SPEC, SMEM_SPEC],
        out_specs=VMEM_SPEC,
        name="mask",
    )(table_row, pair_mask, own_index.reshape(1))


def bias_of(code, small):
    local = jnp.where(code > 0, (code - 1) & (OWNED - 1), -1)
    hot = jnp.where(local == iota(local.shape, 1), 1.0, 0.0).astype(jnp.bfloat16)
    reach = mm(hot, small, ((1,), (1,))).astype(jnp.bfloat16)
    return jnp.where(mm(reach, hot, ((1,), (1,))) > 0.5, 0.0, NEGATIVE)


def squares_body(q_ref, k_ref, out_ref):
    q = q_ref[...].astype(jnp.float32)
    k = k_ref[...].astype(jnp.float32)
    out_ref[0:1, :] = to_row(jnp.sum(q * q, axis=1, keepdims=True))
    out_ref[1:2, :] = to_row(jnp.sum(k * k, axis=1, keepdims=True))
    out_ref[2:8, :] = jnp.zeros((6, TOK), jnp.float32)


def over_head(part):
    return [part] + [lax.ppermute(part, "head", head_perm(d)) for d in (1, 2, 3)]


def total_of(refs):
    return (refs[0][...] + refs[1][...]) + (refs[2][...] + refs[3][...])


def scale_col(total, which):
    return jnp.sqrt(to_col(total[which : which + 1, :]) / WIDTH + EPSILON)


def place_rows(dest_row):
    return jnp.where(iota((SRC_ROWS, TOK), 0) == dest_row, 1.0, 0.0).astype(jnp.bfloat16)


def store_blocks(outs, packed, start):
    width = packed.shape[1]
    cap = packed.shape[0] // len(outs)
    for d, out in enumerate(outs):
        out[:, start : start + width] = packed[d * cap : (d + 1) * cap, :]


def normed(raw, gain, inverse):
    return (raw.astype(jnp.float32) * gain.astype(jnp.float32) * inverse).astype(jnp.bfloat16)


def widths_of(groups):
    return [(hi - lo) * HEAD_DIM for lo, hi in groups]


def pack_body(groups, dest_ref, code_ref, v_ref, g_ref, q_ref, k_ref, gain_ref, *refs):
    total = total_of(refs[:4])
    outs = refs[4:]
    hot = place_rows(dest_ref[...])
    at = 0

    def put(part):
        store_blocks(outs, mm(hot, part, ((1,), (0,))).astype(jnp.bfloat16), at)
        return at + part.shape[1]

    code = jnp.broadcast_to(to_col(code_ref[...]) + 1, (TOK, LANES))
    at = put(code.astype(jnp.float32).astype(jnp.bfloat16))
    sides = [
        (ref, gain, 1.0 / scale_col(total, which))
        for which, (ref, gain) in enumerate(((q_ref, gain_ref[...][0:1]), (k_ref, gain_ref[...][1:2])))
    ]
    for lo, hi in groups:
        cols = slice(lo * HEAD_DIM, hi * HEAD_DIM)
        at = put(v_ref[:, cols])
        at = put(g_ref[:, cols])
        for ref, gain, scale in sides:
            at = put(normed(ref[:, cols], gain[:, cols], scale))


def blocks_of(count, rows, width):
    return (jax.ShapeDtypeStruct((rows, width), jnp.bfloat16),) * count


def pack(groups, count, args):
    width = sum(widths_of(groups)) * 4 + LANES
    return call(
        functools.partial(pack_body, groups),
        blocks_of(count, SRC_ROWS // count, width),
        flops=2 * SRC_ROWS * TOK * width,
        moved=4 * SRC_ROWS * width,
    )(*args)


def z_exchange(blocks, sign):
    return [blocks[0]] + [
        lax.ppermute(blocks[d], "seq", z_perm(sign * d)) for d in range(1, NZ)
    ]


def y_exchange(rows):
    return lax.all_to_all(
        rows, "seq", split_axis=0, concat_axis=0, axis_index_groups=Y_GROUPS, tiled=True
    )


def stacked(blocks, cols):
    if len(blocks) == 1:
        return blocks[0][:, cols]
    return jnp.concatenate([b[:, cols] for b in blocks], axis=0)


def steps_of(width):
    return [slice(a, min(a + 512, width)) for a in range(0, width, 512)]


def spread_body(mode, count_in, cap, z_ref, seen_ref, *refs):
    blocks, outs, table_ref, flag_ref = refs[:count_in], refs[count_in:-2], refs[-2], refs[-1]
    code = stacked(blocks, slice(0, LANES)).astype(jnp.float32).astype(jnp.int32)[:, 0:1]
    if mode == "y":
        key = ((code - 1) >> 2) & (NR - 1)
    else:
        key = (((code - 1) >> 5) - z_ref[0] + NZ) & (NZ - 1)
    key_col = jnp.where(code > 0, key, -1)
    key_row = to_row(key_col)
    square = (SRC_ROWS, SRC_ROWS)
    before = (key_col == key_row) & (iota(square, 0) < iota(square, 1))
    rank_row = jnp.sum(jnp.where(before, jnp.int32(1), jnp.int32(0)), axis=0, keepdims=True)
    dest = jnp.where((key_row >= 0) & (rank_row < cap), key_row * cap + rank_row, -1)
    table_ref[...] = dest
    most = jnp.max(jnp.where(key_row >= 0, rank_row, 0), axis=1, keepdims=True)
    flag_ref[...] = jnp.maximum(seen_ref[...], jnp.where(most < cap, 0.0, 1.0))
    hot = jnp.where(iota((NZ * cap, SRC_ROWS), 0) == dest, 1.0, 0.0).astype(jnp.bfloat16)
    per = 1 if mode == "y" else NZ
    start = 0
    for n in range(0, len(outs), per):
        group = outs[n : n + per]
        width = group[0].shape[1]
        for cols in steps_of(width):
            rows = stacked(blocks, slice(start + cols.start, start + cols.stop))
            store_blocks(group, mm(hot, rows, ((1,), (0,))).astype(jnp.bfloat16), cols.start)
        start += width


def spread(mode, blocks, widths, cap, z_here, seen):
    per = 1 if mode == "y" else NZ
    shapes = sum((blocks_of(per, NZ * cap // per, width) for width in widths), ())
    outs = pl.pallas_call(
        functools.partial(spread_body, mode, len(blocks), cap),
        out_shape=shapes + (jax.ShapeDtypeStruct((1, SRC_ROWS), jnp.int32), FLAG),
        in_specs=[SMEM_SPEC] + [VMEM_SPEC] * (len(blocks) + 1),
        out_specs=(VMEM_SPEC,) * (len(shapes) + 2),
        cost_estimate=pl.CostEstimate(
            flops=2 * NZ * cap * SRC_ROWS * sum(widths), bytes_accessed=0, transcendentals=0
        ),
        compiler_params=pltpu.CompilerParams(vmem_limit_bytes=20 * 1024 * 1024),
    )(z_here.reshape(1), seen, *blocks)
    return [outs[n * per : (n + 1) * per] for n in range(len(widths))], outs[-2], outs[-1]


def gather_body(count, cap, flagged, table_ref, *refs):
    blocks, outs = refs[:count], refs[count:]
    hot = jnp.where(iota((NZ * cap, SRC_ROWS), 0) == table_ref[...], 1.0, 0.0).astype(jnp.bfloat16)
    base = 0
    if flagged:
        base = LANES
        seen = jnp.max(stacked(blocks, slice(0, LANES)).astype(jnp.float32), axis=0, keepdims=True)
        flags = jnp.broadcast_to(seen, (SRC_ROWS, LANES)).astype(jnp.bfloat16)
        store_blocks(outs, flags, 0)
    for cols in steps_of(outs[0].shape[1] - base):
        cols = slice(base + cols.start, base + cols.stop)
        packed = mm(hot, stacked(blocks, cols), ((0,), (0,))).astype(jnp.bfloat16)
        store_blocks(outs, packed, cols.start)


def gather(table, blocks, count_out, cap, flagged):
    width = blocks[0].shape[1]
    return call(
        functools.partial(gather_body, len(blocks), cap, flagged),
        blocks_of(count_out, SRC_ROWS // count_out, width),
        flops=2 * NZ * cap * SRC_ROWS * width,
        moved=4 * NZ * cap * width,
    )(table, *blocks)


def inner_row(grad, raw, gain):
    lifted = grad.astype(jnp.float32) * gain.astype(jnp.float32)
    return to_row(jnp.sum(lifted * raw.astype(jnp.float32), axis=1, keepdims=True))


def unpack_body(groups, flagged, dest_ref, q_ref, k_ref, gain_ref, *refs):
    if flagged:
        other_ref, flag_ref, refs = refs[0], refs[-1], refs[1:-1]
    blocks, outs, inner_ref = refs[:-4], refs[-4:-1], refs[-1]
    hot = place_rows(dest_ref[...])
    sides = (None, (q_ref, gain_ref[...][0:1]), (k_ref, gain_ref[...][1:2]))
    at = 0
    if flagged:
        at = LANES
        inner_ref[...] = other_ref[...]
        seen = [jnp.max(b[:, :LANES].astype(jnp.float32), axis=0, keepdims=True) for b in blocks]
        flag_ref[...] = functools.reduce(jnp.maximum, seen)
    else:
        inner_ref[...] = jnp.zeros((8, TOK), jnp.float32)
    for lo, hi in groups:
        width = (hi - lo) * HEAD_DIM
        cols = slice(lo * HEAD_DIM, hi * HEAD_DIM)
        base = (lo - groups[0][0]) * HEAD_DIM
        for n, (out, side) in enumerate(zip(outs, sides)):
            grad = mm(hot, stacked(blocks, slice(at, at + width)), ((0,), (0,))).astype(jnp.bfloat16)
            at += width
            out[:, base : base + width] = grad
            if side is not None:
                inner_ref[n - 1 : n, :] += inner_row(grad, side[0][:, cols], side[1][:, cols])


def unpack(groups, dest, sides, blocks, other=None):
    width = sum(widths_of(groups))
    flagged = other is not None
    return call(
        functools.partial(unpack_body, groups, flagged),
        blocks_of(3, TOK, width)
        + (jax.ShapeDtypeStruct((8, TOK), jnp.float32),)
        + ((FLAG,) if flagged else ()),
        flops=2 * SRC_ROWS * TOK * width * 3,
        moved=4 * SRC_ROWS * width * 3,
    )(dest, *sides, *((other,) if flagged else ()), *blocks)


def attend_body(heads, count, flagged, mask_ref, *refs):
    if flagged:
        flag_ref, refs = refs[0], refs[1:]
    blocks, outs = refs[:count], refs[count : 2 * count]
    scratch = list(refs[2 * count :])
    bias_ref, probs_ref, grads_ref = scratch[:3]
    rows, width = bias_ref.shape[0], heads * HEAD_DIM
    base = LANES if flagged else 0
    if count == 1:
        data, result = blocks[0], outs[0]
    else:
        data, result = scratch[3:]
        cap = rows // count
        for d, block in enumerate(blocks):
            data[d * cap : (d + 1) * cap, :] = block[...]
    inv = 1.0 / math.sqrt(HEAD_DIM)
    bias_ref[...] = bias_of(data[:, :LANES].astype(jnp.float32).astype(jnp.int32), mask_ref[...])
    if flagged:
        result[:, :LANES] = jnp.broadcast_to(flag_ref[...], (rows, LANES)).astype(jnp.bfloat16)

    def one_head(h, carry):
        v_ref, g_ref, q_ref, k_ref = (
            data.at[:, pl.ds(pl.multiple_of(LANES + n * width + h * HEAD_DIM, HEAD_DIM), HEAD_DIM)]
            for n in range(4)
        )
        keys = k_ref[...]
        vals = v_ref[...]
        for a in range(0, rows, LANES):
            part = slice(a, min(a + LANES, rows))
            scores = mm(keys, q_ref[part, :], ((1,), (1,))) * inv + bias_ref[:, part]
            raised = jnp.exp(scores - jnp.max(scores, axis=0, keepdims=True))
            probs = raised * (1.0 / jnp.sum(raised, axis=0, keepdims=True))
            low = probs.astype(jnp.bfloat16)
            gp = mm(vals, g_ref[part, :], ((1,), (1,)))
            delta = jnp.sum(low.astype(jnp.float32) * gp, axis=0, keepdims=True)
            probs_ref[:, part] = low
            grads_ref[:, part] = (probs * (gp - delta) * inv).astype(jnp.bfloat16)
        gs = grads_ref[...]
        grads = (
            mm(probs_ref[...], g_ref[...], ((1,), (0,))),
            mm(gs, keys, ((0,), (0,))),
            mm(gs, q_ref[...], ((1,), (0,))),
        )
        for n, res in enumerate(grads):
            at = pl.multiple_of(base + n * width + h * HEAD_DIM, HEAD_DIM)
            result[:, pl.ds(at, HEAD_DIM)] = res.astype(jnp.bfloat16)
        return carry

    lax.fori_loop(0, heads, one_head, 0)
    if count > 1:
        store_blocks(outs, result[...], 0)


def attend(mask, blocks, heads, flag=None):
    count = len(blocks)
    rows = count * blocks[0].shape[0]
    flagged = flag is not None
    width = 3 * heads * HEAD_DIM + (LANES if flagged else 0)
    square = (rows, rows)
    scratch = [pltpu.VMEM(square, kind) for kind in (jnp.float32, jnp.bfloat16, jnp.bfloat16)]
    if count > 1:
        scratch.append(pltpu.VMEM((rows, blocks[0].shape[1]), jnp.bfloat16))
        scratch.append(pltpu.VMEM((rows, width), jnp.bfloat16))
    return call(
        functools.partial(attend_body, heads, count, flagged),
        blocks_of(count, rows // count, width),
        flops=20 * rows * rows * HEAD_DIM * heads,
        moved=14 * rows * heads * HEAD_DIM,
        scratch=scratch,
    )(mask, *((flag,) if flagged else ()), *blocks)


def finish_body(*refs):
    va, qa, ka, vb, qb, kb, q_ref, k_ref, gain_ref = refs[:9]
    squares = total_of(refs[9:13])
    inners = total_of(refs[13:17])
    gq_ref, gk_ref, gv_ref = refs[17:]
    spans = (slice(0, SPLIT), slice(SPLIT, WIDTH_HERE))
    sides = (((qa, qb), q_ref, gq_ref), ((ka, kb), k_ref, gk_ref))
    for n, (pieces, x, out) in enumerate(sides):
        scale = scale_col(squares, n)
        inner = to_col(inners[n : n + 1, :])
        slope = inner / (WIDTH * scale * scale * scale)
        inverse = 1.0 / scale
        for piece, cols in zip(pieces, spans):
            lifted = piece[...].astype(jnp.float32) * gain_ref[...][n : n + 1, cols]
            result = lifted * inverse - x[:, cols].astype(jnp.float32) * slope
            out[:, cols] = result.astype(jnp.bfloat16)
    for piece, cols in zip((va, vb), spans):
        gv_ref[:, cols] = piece[...]


FULL = 64 * OWNED * 2
TILE = pl.BlockSpec((TOK, HEAD_DIM), lambda n: (0, n))


def fixed(shape):
    return pl.BlockSpec(shape, lambda n: (0, 0))


def stack_tile(count, rows):
    return pl.BlockSpec((count, rows, HEAD_DIM), lambda n: (0, 0, n))


def full_slots(slot_row):
    return jnp.where(iota((FULL, TOK), 0) == slot_row, 1.0, 0.0).astype(jnp.bfloat16)


def full_pack_body(slot_ref, *refs):
    hot = full_slots(slot_ref[...])
    for n, ref in enumerate(refs[:4]):
        refs[4][n] = mm(hot, ref[...], ((1,), (0,))).astype(jnp.bfloat16)


def full_unpack_body(slot_ref, in_ref, out_ref):
    hot = full_slots(slot_ref[...])
    for n in range(3):
        out_ref[n] = mm(hot, in_ref[n], ((0,), (0,))).astype(jnp.bfloat16)


def full_attend_body(mask_ref, code_ref, in_ref, out_ref):
    inv = 1.0 / math.sqrt(HEAD_DIM)
    q, k, v, g = (in_ref[n] for n in range(4))
    scores = mm(k, q, ((1,), (1,))) * inv + bias_of(code_ref[...], mask_ref[...])
    raised = jnp.exp(scores - jnp.max(scores, axis=0, keepdims=True))
    probs = raised / jnp.sum(raised, axis=0, keepdims=True)
    low = probs.astype(jnp.bfloat16)
    gp = mm(v, g, ((1,), (1,)))
    delta = jnp.sum(low.astype(jnp.float32) * gp, axis=0, keepdims=True)
    gs = (probs * (gp - delta) * inv).astype(jnp.bfloat16)
    out_ref[0] = mm(gs, k, ((0,), (0,))).astype(jnp.bfloat16)
    out_ref[1] = mm(gs, q, ((1,), (0,))).astype(jnp.bfloat16)
    out_ref[2] = mm(low, g, ((1,), (0,))).astype(jnp.bfloat16)


def by_head(body, ins, specs, count, rows):
    return pl.pallas_call(
        body,
        grid=(HEADS_HERE,),
        out_shape=jax.ShapeDtypeStruct((count, rows, WIDTH_HERE), jnp.bfloat16),
        in_specs=specs,
        out_specs=stack_tile(count, rows),
        compiler_params=pltpu.CompilerParams(vmem_limit_bytes=20 * 1024 * 1024),
    )(*ins)


def full_exchange(q_norm, k_norm, values, grad_out, code_row, own_index, small):
    square = (TOK, TOK)
    code_col = code_row.reshape(TOK, 1)
    same = (code_col == code_row) & (iota(square, 0) < iota(square, 1))
    slot_row = code_row * 2 + jnp.sum(same.astype(jnp.int32), axis=0, keepdims=True)
    codes = lax.all_to_all(
        jnp.broadcast_to(code_row, (NZ * NR, TOK)), "seq", split_axis=0, concat_axis=0, tiled=True
    )
    slots_here = jnp.arange(OWNED, dtype=jnp.int32) + own_index * OWNED
    held = jnp.sum((codes[:, None, :] == slots_here[None, :, None]).astype(jnp.int32), axis=2)
    live = held[:, :, None] > jnp.arange(2, dtype=jnp.int32)[None, None, :]
    rows = jnp.where(live, jnp.arange(1, OWNED + 1, dtype=jnp.int32)[None, :, None], 0)
    code = jnp.broadcast_to(rows.reshape(FULL, 1), (FULL, LANES))

    def swap(array):
        return lax.all_to_all(array, "seq", split_axis=0, concat_axis=0, tiled=True)

    row = fixed((1, TOK))
    raws = (q_norm, k_norm, values, grad_out)
    sent = by_head(full_pack_body, (slot_row, *raws), [row] + [TILE] * 4, 4, FULL)
    arrived = lax.map(swap, sent)
    grads = by_head(
        full_attend_body,
        (small, code, arrived),
        [fixed((LANES, LANES)), fixed((FULL, LANES)), stack_tile(4, FULL)],
        3,
        FULL,
    )
    home = lax.map(swap, grads)
    rows = by_head(full_unpack_body, (slot_row, home), [row, stack_tile(3, FULL)], 3, TOK)
    return rows[0], rows[1], rows[2]


def on_device(
    query_raw, key_raw, values, grad_out, query_gain, key_gain, cluster_of, pair_mask, cluster_owner
):
    own_index = lax.axis_index("seq").astype(jnp.int32)
    z_here = own_index // NR
    gains = jnp.stack([query_gain, key_gain]).astype(jnp.float32)
    table_row, code_row, dest_a, dest_b, flag = prep(cluster_of, cluster_owner, z_here)
    row_sums = jax.ShapeDtypeStruct((8, TOK), jnp.float32)
    norms = over_head(call(squares_body, row_sums)(query_raw, key_raw))
    raw_args = (code_row, values, grad_out, query_raw, key_raw, gains, *norms)

    a_packed = pack(GROUPS_A, NZ, (dest_a, *raw_args))
    a_sent = z_exchange(a_packed, 1)
    (b_packed,) = pack(GROUPS_B, 1, (dest_b, *raw_args))
    b_middle = y_exchange(b_packed)
    small = small_mask(table_row, pair_mask, own_index)

    (a_wide,), (b_wide,) = widths_of(GROUPS_A), widths_of(GROUPS_B)
    (b_blocks,), b_table, flag = spread(
        "z", (b_middle,), (LANES + 4 * b_wide,), Z_CAP, z_here, flag
    )
    b_arrived = z_exchange(b_blocks, 1)
    ((a_rows,),), a_table, flag = spread("y", a_sent, (LANES + 4 * a_wide,), Y_CAP, z_here, flag)
    a_arrived = y_exchange(a_rows)
    (a_grads,) = attend(small, (a_arrived,), a_wide // HEAD_DIM, flag)
    a_back = y_exchange(a_grads)
    b_grads = attend(small, b_arrived, b_wide // HEAD_DIM)
    b_return = z_exchange(b_grads, -1)
    a_blocks = gather(a_table, (a_back,), NZ, Y_CAP, True)
    a_return = z_exchange(a_blocks, -1)
    (b_rows,) = gather(b_table, b_return, 1, Z_CAP, False)
    b_home = y_exchange(b_rows)
    sides = (query_raw, key_raw, gains)
    *home_b, inner_b = unpack(GROUPS_B, dest_b, sides, (b_home,))
    *home_a, inner, overflow = unpack(GROUPS_A, dest_a, sides, a_return, inner_b)
    given = (*norms, query_raw, key_raw, values, grad_out, gains, code_row, small)

    def slow(state):
        trip, inputs = lax.optimization_barrier((state[0], given))
        return redo(trip, *inputs)

    def redo(trip, n0, n1, n2, n3, query_raw, key_raw, values, grad_out, gains, code_row, small):
        squares = (n0 + n1) + (n2 + n3)
        scales = jnp.sqrt(squares / WIDTH + EPSILON)
        q_norm = normed(query_raw, gains[0:1], 1.0 / scales[0][:, None])
        k_norm = normed(key_raw, gains[1:2], 1.0 / scales[1][:, None])
        home_q, home_k, home_v = full_exchange(
            q_norm, k_norm, values, grad_out, code_row, own_index, small
        )
        parts = [
            jnp.sum(h.astype(jnp.float32) * g.astype(jnp.float32) * x.astype(jnp.float32), axis=1)
            for h, g, x in ((home_q, gains[0:1], query_raw), (home_k, gains[1:2], key_raw))
        ]
        rows = jnp.concatenate([jnp.stack(parts), jnp.zeros((6, TOK), jnp.float32)])
        homes = (home_v, home_q, home_k)
        return (
            trip + 1.0,
            tuple(h[:, :SPLIT] for h in homes),
            tuple(h[:, SPLIT:] for h in homes),
            rows,
        )

    trips = overflow[0, 0]
    _, home_a, home_b, inner = lax.while_loop(
        lambda state: state[0] < trips,
        slow,
        (jnp.float32(0), tuple(home_a), tuple(home_b), inner),
    )
    inners = over_head(inner)
    out = jax.ShapeDtypeStruct((TOK, WIDTH_HERE), jnp.bfloat16)
    return call(finish_body, (out,) * 3)(*home_a, *home_b, *sides, *norms, *inners)


def solution(mesh):
    return jax.shard_map(
        on_device,
        mesh=mesh,
        in_specs=(
            P("seq", "head"),
            P("seq", "head"),
            P("seq", "head"),
            P("seq", "head"),
            P("head"),
            P("head"),
            P("seq"),
            P(),
            P(),
        ),
        out_specs=(P("seq", "head"), P("seq", "head"), P("seq", "head")),
        check_vma=False,
    )
```

```python
import functools
import math

import jax
import jax.numpy as jnp
from jax import lax
from jax.experimental import pallas as pl
from jax.experimental.pallas import tpu as pltpu
from jax.sharding import PartitionSpec as P


WIDTH = 5120
HEAD_DIM = 128
EPSILON = 1e-06
NEGATIVE = -1e30

TOK = 256
NZ = 8
NR = 8
OWNED = 4
SRC_CAP = 48
Y_CAP = 56
Z_CAP = 56
SRC_ROWS = NZ * SRC_CAP
WIDTH_HERE = 1280
HEADS_HERE = 10
GROUPS_A = ((0, 5),)
GROUPS_B = ((5, 10),)
SPLIT = 5 * HEAD_DIM
LANES = 128


Y_GROUPS = [[NR * z + r for r in range(NR)] for z in range(NZ)]


def z_perm(shift):
    return [(s, ((s // NR + shift) % NZ) * NR + s % NR) for s in range(NZ * NR)]


def head_perm(shift):
    return [(s, (s + shift) % 4) for s in range(4)]


def call(body, out_shape, flops=0, moved=0, scratch=()):
    return pl.pallas_call(
        body,
        out_shape=out_shape,
        scratch_shapes=scratch,
        cost_estimate=pl.CostEstimate(flops=flops, bytes_accessed=moved, transcendentals=0),
        compiler_params=pltpu.CompilerParams(vmem_limit_bytes=20 * 1024 * 1024),
    )


def iota(shape, dim):
    return lax.broadcasted_iota(jnp.int32, shape, dim)


def to_col(row):
    n = row.shape[1]
    eye = iota((n, n), 0) == iota((n, n), 1)
    return jnp.sum(jnp.where(eye, jnp.broadcast_to(row, (n, n)), jnp.zeros((), row.dtype)), axis=1, keepdims=True)


def to_row(col):
    n = col.shape[0]
    eye = iota((n, n), 0) == iota((n, n), 1)
    return jnp.sum(jnp.where(eye, jnp.broadcast_to(col, (n, n)), jnp.zeros((), col.dtype)), axis=0, keepdims=True)


def mm(a, b, dims):
    return lax.dot_general(a, b, (dims, ((), ())), preferred_element_type=jnp.float32)


def prep_body(cluster_ref, owner_ref, z_ref, table_ref, code_ref, dest_a_ref, dest_b_ref, flag_ref):
    square = (TOK, TOK)
    owner_row = owner_ref[...]
    owner_col = to_col(owner_row)
    earlier = iota(square, 0) < iota(square, 1)
    one, zero = jnp.int32(1), jnp.int32(0)
    local_row = jnp.sum(
        jnp.where((owner_col == owner_row) & earlier, one, zero), axis=0, keepdims=True
    )
    table_row = owner_row * OWNED + local_row
    table_ref[...] = table_row
    table_col = to_col(table_row)
    code_row = jnp.sum(
        jnp.where(iota(square, 0) == cluster_ref[...], table_col, zero), axis=0, keepdims=True
    )
    code_ref[...] = code_row
    ranks = []
    for key_row, out_ref in (
        (((code_row >> 5) - z_ref[0] + NZ) & (NZ - 1), dest_a_ref),
        ((code_row >> 2) & (NR - 1), dest_b_ref),
    ):
        key_col = to_col(key_row)
        rank_row = jnp.sum(
            jnp.where((key_col == key_row) & earlier, one, zero), axis=0, keepdims=True
        )
        out_ref[...] = jnp.where(rank_row < SRC_CAP, key_row * SRC_CAP + rank_row, -1)
        ranks.append(rank_row)
    most = jnp.max(jnp.maximum(ranks[0], ranks[1]), axis=1, keepdims=True)
    flag_ref[...] = jnp.broadcast_to(jnp.where(most < SRC_CAP, 0.0, 1.0), (1, LANES))


FLAG = jax.ShapeDtypeStruct((1, LANES), jnp.float32)
VMEM_SPEC = pl.BlockSpec(memory_space=pltpu.VMEM)
SMEM_SPEC = pl.BlockSpec(memory_space=pltpu.SMEM)


def prep(cluster_of, cluster_owner, z_here):
    row = jax.ShapeDtypeStruct((1, TOK), jnp.int32)
    return pl.pallas_call(
        prep_body,
        out_shape=(row,) * 4 + (FLAG,),
        in_specs=[VMEM_SPEC, VMEM_SPEC, SMEM_SPEC],
        out_specs=(VMEM_SPEC,) * 5,
        name="prep",
    )(cluster_of.reshape(1, TOK), cluster_owner.reshape(1, TOK), z_here.reshape(1))


def mask_body(table_ref, mask_ref, own_ref, out_ref):
    slots = iota((LANES, TOK), 0)
    chosen = (table_ref[...] == own_ref[0] * OWNED + slots) & (slots < OWNED)
    chosen = jnp.where(chosen, 1.0, 0.0).astype(jnp.bfloat16)
    pairs = mask_ref[...].astype(jnp.float32).astype(jnp.bfloat16)
    rows = mm(chosen, pairs, ((1,), (0,))).astype(jnp.bfloat16)
    out_ref[...] = mm(rows, chosen, ((1,), (1,))).astype(jnp.bfloat16)


def small_mask(table_row, pair_mask, own_index):
    return pl.pallas_call(
        mask_body,
        out_shape=jax.ShapeDtypeStruct((LANES, LANES), jnp.bfloat16),
        in_specs=[VMEM_SPEC, VMEM_SPEC, SMEM_SPEC],
        out_specs=VMEM_SPEC,
        name="mask",
    )(table_row, pair_mask, own_index.reshape(1))


def bias_of(code, small):
    local = jnp.where(code > 0, (code - 1) & (OWNED - 1), -1)
    hot = jnp.where(local == iota(local.shape, 1), 1.0, 0.0).astype(jnp.bfloat16)
    reach = mm(hot, small, ((1,), (1,))).astype(jnp.bfloat16)
    return jnp.where(mm(reach, hot, ((1,), (1,))) > 0.5, 0.0, NEGATIVE)


def squares_body(q_ref, k_ref, out_ref):
    q = q_ref[...].astype(jnp.float32)
    k = k_ref[...].astype(jnp.float32)
    out_ref[0:1, :] = to_row(jnp.sum(q * q, axis=1, keepdims=True))
    out_ref[1:2, :] = to_row(jnp.sum(k * k, axis=1, keepdims=True))
    out_ref[2:8, :] = jnp.zeros((6, TOK), jnp.float32)


def over_head(part):
    return [part] + [lax.ppermute(part, "head", head_perm(d)) for d in (1, 2, 3)]


def total_of(refs):
    return (refs[0][...] + refs[1][...]) + (refs[2][...] + refs[3][...])


def scale_col(total, which):
    return jnp.sqrt(to_col(total[which : which + 1, :]) / WIDTH + EPSILON)


def place_rows(dest_row):
    return jnp.where(iota((SRC_ROWS, TOK), 0) == dest_row, 1.0, 0.0).astype(jnp.bfloat16)


def store_blocks(outs, packed, start):
    width = packed.shape[1]
    cap = packed.shape[0] // len(outs)
    for d, out in enumerate(outs):
        out[:, start : start + width] = packed[d * cap : (d + 1) * cap, :]


def normed(raw, gain, inverse):
    return (raw.astype(jnp.float32) * gain.astype(jnp.float32) * inverse).astype(jnp.bfloat16)


def widths_of(groups):
    return [(hi - lo) * HEAD_DIM for lo, hi in groups]


def pack_body(groups, dest_ref, code_ref, v_ref, g_ref, q_ref, k_ref, gain_ref, *refs):
    total = total_of(refs[:4])
    outs = refs[4:]
    hot = place_rows(dest_ref[...])
    at = 0

    def put(part):
        store_blocks(outs, mm(hot, part, ((1,), (0,))).astype(jnp.bfloat16), at)
        return at + part.shape[1]

    code = jnp.broadcast_to(to_col(code_ref[...]) + 1, (TOK, LANES))
    at = put(code.astype(jnp.float32).astype(jnp.bfloat16))
    sides = [
        (ref, gain, 1.0 / scale_col(total, which))
        for which, (ref, gain) in enumerate(((q_ref, gain_ref[...][0:1]), (k_ref, gain_ref[...][1:2])))
    ]
    for lo, hi in groups:
        cols = slice(lo * HEAD_DIM, hi * HEAD_DIM)
        at = put(v_ref[:, cols])
        at = put(g_ref[:, cols])
        for ref, gain, scale in sides:
            at = put(normed(ref[:, cols], gain[:, cols], scale))


def blocks_of(count, rows, width):
    return (jax.ShapeDtypeStruct((rows, width), jnp.bfloat16),) * count


def pack(groups, count, args):
    width = sum(widths_of(groups)) * 4 + LANES
    return call(
        functools.partial(pack_body, groups),
        blocks_of(count, SRC_ROWS // count, width),
        flops=2 * SRC_ROWS * TOK * width,
        moved=4 * SRC_ROWS * width,
    )(*args)


FAR = (4, 3, 5)
NEAR = (2, 6, 1, 7)


def z_exchange(blocks, sign):
    got = {0: blocks[0]}
    for shifts in (FAR, NEAR):
        for d in shifts:
            got[d] = lax.ppermute(blocks[d], "seq", z_perm(sign * d))
    return [got[d] for d in range(NZ)]


def y_exchange(rows):
    return lax.all_to_all(
        rows, "seq", split_axis=0, concat_axis=0, axis_index_groups=Y_GROUPS, tiled=True
    )


def stacked(blocks, cols):
    if len(blocks) == 1:
        return blocks[0][:, cols]
    return jnp.concatenate([b[:, cols] for b in blocks], axis=0)


def steps_of(width):
    return [slice(a, min(a + 512, width)) for a in range(0, width, 512)]


def spread_body(mode, count_in, cap, z_ref, seen_ref, *refs):
    blocks, outs, table_ref, flag_ref = refs[:count_in], refs[count_in:-2], refs[-2], refs[-1]
    code = stacked(blocks, slice(0, LANES)).astype(jnp.float32).astype(jnp.int32)[:, 0:1]
    if mode == "y":
        key = ((code - 1) >> 2) & (NR - 1)
    else:
        key = (((code - 1) >> 5) - z_ref[0] + NZ) & (NZ - 1)
    key_col = jnp.where(code > 0, key, -1)
    key_row = to_row(key_col)
    square = (SRC_ROWS, SRC_ROWS)
    before = (key_col == key_row) & (iota(square, 0) < iota(square, 1))
    rank_row = jnp.sum(jnp.where(before, jnp.int32(1), jnp.int32(0)), axis=0, keepdims=True)
    dest = jnp.where((key_row >= 0) & (rank_row < cap), key_row * cap + rank_row, -1)
    table_ref[...] = dest
    most = jnp.max(jnp.where(key_row >= 0, rank_row, 0), axis=1, keepdims=True)
    flag_ref[...] = jnp.maximum(seen_ref[...], jnp.where(most < cap, 0.0, 1.0))
    hot = jnp.where(iota((NZ * cap, SRC_ROWS), 0) == dest, 1.0, 0.0).astype(jnp.bfloat16)
    per = 1 if mode == "y" else NZ
    start = 0
    for n in range(0, len(outs), per):
        group = outs[n : n + per]
        width = group[0].shape[1]
        for cols in steps_of(width):
            rows = stacked(blocks, slice(start + cols.start, start + cols.stop))
            store_blocks(group, mm(hot, rows, ((1,), (0,))).astype(jnp.bfloat16), cols.start)
        start += width


def spread(mode, blocks, widths, cap, z_here, seen):
    per = 1 if mode == "y" else NZ
    shapes = sum((blocks_of(per, NZ * cap // per, width) for width in widths), ())
    outs = pl.pallas_call(
        functools.partial(spread_body, mode, len(blocks), cap),
        out_shape=shapes + (jax.ShapeDtypeStruct((1, SRC_ROWS), jnp.int32), FLAG),
        in_specs=[SMEM_SPEC] + [VMEM_SPEC] * (len(blocks) + 1),
        out_specs=(VMEM_SPEC,) * (len(shapes) + 2),
        cost_estimate=pl.CostEstimate(
            flops=2 * NZ * cap * SRC_ROWS * sum(widths), bytes_accessed=0, transcendentals=0
        ),
        compiler_params=pltpu.CompilerParams(vmem_limit_bytes=20 * 1024 * 1024),
    )(z_here.reshape(1), seen, *blocks)
    return [outs[n * per : (n + 1) * per] for n in range(len(widths))], outs[-2], outs[-1]


def gather_body(count, cap, flagged, table_ref, *refs):
    blocks, outs = refs[:count], refs[count:]
    hot = jnp.where(iota((NZ * cap, SRC_ROWS), 0) == table_ref[...], 1.0, 0.0).astype(jnp.bfloat16)
    base = 0
    if flagged:
        base = LANES
        seen = jnp.max(stacked(blocks, slice(0, LANES)).astype(jnp.float32), axis=0, keepdims=True)
        flags = jnp.broadcast_to(seen, (SRC_ROWS, LANES)).astype(jnp.bfloat16)
        store_blocks(outs, flags, 0)
    for cols in steps_of(outs[0].shape[1] - base):
        cols = slice(base + cols.start, base + cols.stop)
        packed = mm(hot, stacked(blocks, cols), ((0,), (0,))).astype(jnp.bfloat16)
        store_blocks(outs, packed, cols.start)


def gather(table, blocks, count_out, cap, flagged):
    width = blocks[0].shape[1]
    return call(
        functools.partial(gather_body, len(blocks), cap, flagged),
        blocks_of(count_out, SRC_ROWS // count_out, width),
        flops=2 * NZ * cap * SRC_ROWS * width,
        moved=4 * NZ * cap * width,
    )(table, *blocks)


def inner_row(grad, raw, gain):
    lifted = grad.astype(jnp.float32) * gain.astype(jnp.float32)
    return to_row(jnp.sum(lifted * raw.astype(jnp.float32), axis=1, keepdims=True))


def unpack_body(groups, flagged, dest_ref, q_ref, k_ref, gain_ref, *refs):
    if flagged:
        other_ref, flag_ref, refs = refs[0], refs[-1], refs[1:-1]
    blocks, outs, inner_ref = refs[:-4], refs[-4:-1], refs[-1]
    hot = place_rows(dest_ref[...])
    sides = (None, (q_ref, gain_ref[...][0:1]), (k_ref, gain_ref[...][1:2]))
    at = 0
    if flagged:
        at = LANES
        inner_ref[...] = other_ref[...]
        seen = [jnp.max(b[:, :LANES].astype(jnp.float32), axis=0, keepdims=True) for b in blocks]
        flag_ref[...] = functools.reduce(jnp.maximum, seen)
    else:
        inner_ref[...] = jnp.zeros((8, TOK), jnp.float32)
    for lo, hi in groups:
        width = (hi - lo) * HEAD_DIM
        cols = slice(lo * HEAD_DIM, hi * HEAD_DIM)
        base = (lo - groups[0][0]) * HEAD_DIM
        for n, (out, side) in enumerate(zip(outs, sides)):
            grad = mm(hot, stacked(blocks, slice(at, at + width)), ((0,), (0,))).astype(jnp.bfloat16)
            at += width
            out[:, base : base + width] = grad
            if side is not None:
                inner_ref[n - 1 : n, :] += inner_row(grad, side[0][:, cols], side[1][:, cols])


def unpack(groups, dest, sides, blocks, other=None):
    width = sum(widths_of(groups))
    flagged = other is not None
    return call(
        functools.partial(unpack_body, groups, flagged),
        blocks_of(3, TOK, width)
        + (jax.ShapeDtypeStruct((8, TOK), jnp.float32),)
        + ((FLAG,) if flagged else ()),
        flops=2 * SRC_ROWS * TOK * width * 3,
        moved=4 * SRC_ROWS * width * 3,
    )(dest, *sides, *((other,) if flagged else ()), *blocks)


def at_head(start, h):
    return pl.ds(pl.multiple_of(start + h * HEAD_DIM, HEAD_DIM), HEAD_DIM)


def one_head(v_ref, g_ref, q_ref, k_ref, bias_ref, probs_ref, grads_ref, outs, unroll):
    rows = bias_ref.shape[0]
    inv = 1.0 / math.sqrt(HEAD_DIM)

    def one_part(part):
        scores = mm(k_ref[...], q_ref[part, :], ((1,), (1,))) * inv + bias_ref[:, part]
        raised = jnp.exp(scores - jnp.max(scores, axis=0, keepdims=True))
        probs = raised * (1.0 / jnp.sum(raised, axis=0, keepdims=True))
        low = probs.astype(jnp.bfloat16)
        gp = mm(v_ref[...], g_ref[part, :], ((1,), (1,)))
        delta = jnp.sum(low.astype(jnp.float32) * gp, axis=0, keepdims=True)
        probs_ref[:, part] = low
        grads_ref[:, part] = (probs * (gp - delta) * inv).astype(jnp.bfloat16)

    if unroll:
        for a in range(0, rows, LANES):
            one_part(slice(a, min(a + LANES, rows)))
    else:

        def step(n, carry):
            one_part(pl.ds(pl.multiple_of(n * LANES, LANES), LANES))
            return carry

        lax.fori_loop(0, rows // LANES, step, 0)
    gs = grads_ref[...]
    outs[0][...] = mm(probs_ref[...], g_ref[...], ((1,), (0,))).astype(jnp.bfloat16)
    outs[1][...] = mm(gs, k_ref[...], ((0,), (0,))).astype(jnp.bfloat16)
    outs[2][...] = mm(gs, q_ref[...], ((1,), (0,))).astype(jnp.bfloat16)


def attend_body(heads, count, flagged, mask_ref, *refs):
    if flagged:
        flag_ref, refs = refs[0], refs[1:]
    blocks, outs = refs[:count], refs[count : 2 * count]
    bias_ref, probs_ref, grads_ref = refs[2 * count : 2 * count + 3]
    rows, width = bias_ref.shape[0], heads * HEAD_DIM
    base = LANES if flagged else 0
    if count == 1:
        data, result = blocks[0], outs[0]
    else:
        data, result = refs[2 * count + 3 :]
        cap = rows // count
        for d, block in enumerate(blocks):
            data[d * cap : (d + 1) * cap, :] = block[...]
    bias_ref[...] = bias_of(data[:, :LANES].astype(jnp.float32).astype(jnp.int32), mask_ref[...])
    if flagged:
        result[:, :LANES] = jnp.broadcast_to(flag_ref[...], (rows, LANES)).astype(jnp.bfloat16)

    def step(h, carry):
        ins = [data.at[:, at_head(LANES + n * width, h)] for n in range(4)]
        grads = [result.at[:, at_head(base + n * width, h)] for n in range(3)]
        one_head(*ins, bias_ref, probs_ref, grads_ref, grads, True)
        return carry

    lax.fori_loop(0, heads, step, 0)
    if count > 1:
        store_blocks(outs, result[...], 0)


def attend(mask, blocks, heads, flag=None):
    count = len(blocks)
    rows = count * blocks[0].shape[0]
    flagged = flag is not None
    width = 3 * heads * HEAD_DIM + (LANES if flagged else 0)
    square = (rows, rows)
    scratch = [pltpu.VMEM(square, kind) for kind in (jnp.float32, jnp.bfloat16, jnp.bfloat16)]
    if count > 1:
        scratch.append(pltpu.VMEM((rows, blocks[0].shape[1]), jnp.bfloat16))
        scratch.append(pltpu.VMEM((rows, width), jnp.bfloat16))
    return call(
        functools.partial(attend_body, heads, count, flagged),
        blocks_of(count, rows // count, width),
        flops=20 * rows * rows * HEAD_DIM * heads,
        moved=14 * rows * heads * HEAD_DIM,
        scratch=scratch,
    )(mask, *((flag,) if flagged else ()), *blocks)


def finish_body(*refs):
    va, qa, ka, vb, qb, kb, q_ref, k_ref, gain_ref = refs[:9]
    squares = total_of(refs[9:13])
    inners = total_of(refs[13:17])
    gq_ref, gk_ref, gv_ref = refs[17:]
    spans = (slice(0, SPLIT), slice(SPLIT, WIDTH_HERE))
    sides = (((qa, qb), q_ref, gq_ref), ((ka, kb), k_ref, gk_ref))
    for n, (pieces, x, out) in enumerate(sides):
        scale = scale_col(squares, n)
        inner = to_col(inners[n : n + 1, :])
        slope = inner / (WIDTH * scale * scale * scale)
        inverse = 1.0 / scale
        for piece, cols in zip(pieces, spans):
            lifted = piece[...].astype(jnp.float32) * gain_ref[...][n : n + 1, cols]
            result = lifted * inverse - x[:, cols].astype(jnp.float32) * slope
            out[:, cols] = result.astype(jnp.bfloat16)
    for piece, cols in zip((va, vb), spans):
        gv_ref[:, cols] = piece[...]


FULL = 64 * OWNED * 2
TILE = pl.BlockSpec((TOK, HEAD_DIM), lambda n: (0, n))


def fixed(shape):
    return pl.BlockSpec(shape, lambda n: (0, 0))


def stack_tile(count, rows):
    return pl.BlockSpec((count, rows, HEAD_DIM), lambda n: (0, 0, n))


def full_slots(code_ref):
    code_row = code_ref[...]
    square = (TOK, TOK)
    same = (to_col(code_row) == code_row) & (iota(square, 0) < iota(square, 1))
    rank = jnp.sum(jnp.where(same, jnp.int32(1), jnp.int32(0)), axis=0, keepdims=True)
    return jnp.where(iota((FULL, TOK), 0) == code_row * 2 + rank, 1.0, 0.0).astype(jnp.bfloat16)


def full_pack_body(code_ref, v_ref, g_ref, q_ref, k_ref, gain_ref, *refs):
    total, out_ref = total_of(refs[:4]), refs[4]
    parts = [v_ref[...], g_ref[...]]
    for n, ref in enumerate((q_ref, k_ref)):
        parts.append(normed(ref[...], gain_ref[...][n : n + 1], 1.0 / scale_col(total, n)))
    parts.append(jnp.ones((TOK, HEAD_DIM), jnp.bfloat16))
    packed = mm(full_slots(code_ref), jnp.concatenate(parts, axis=1), ((1,), (0,))).astype(jnp.bfloat16)
    for n in range(5):
        out_ref[n] = packed[:, n * HEAD_DIM : (n + 1) * HEAD_DIM]


def full_unpack_body(code_ref, q_ref, k_ref, gain_ref, in_ref, out_ref, inner_ref):
    rows = jnp.concatenate([in_ref[n] for n in range(3)], axis=1)
    grads = mm(full_slots(code_ref), rows, ((0,), (0,))).astype(jnp.bfloat16)

    @pl.when(pl.program_id(0) == 0)
    def _():
        inner_ref[...] = jnp.zeros((8, TOK), jnp.float32)

    for n, ref in enumerate((None, q_ref, k_ref)):
        grad = grads[:, n * HEAD_DIM : (n + 1) * HEAD_DIM]
        out_ref[n] = grad
        if n > 0:
            lifted = grad.astype(jnp.float32) * gain_ref[...][n - 1 : n]
            part = jnp.sum(lifted * ref[...].astype(jnp.float32), axis=1, keepdims=True)
            inner_ref[n - 1 : n, :] += to_row(part)


def full_attend_body(mask_ref, in_ref, out_ref, bias_ref, probs_ref, grads_ref):
    @pl.when(pl.program_id(0) == 0)
    def _():
        live = in_ref[4].astype(jnp.float32) > 0.5
        bias_ref[...] = bias_of(jnp.where(live, ((iota((FULL, LANES), 0) >> 1) & 3) + 1, 0), mask_ref[...])

    one_head(*(in_ref.at[n] for n in range(4)), bias_ref, probs_ref, grads_ref, [out_ref.at[n] for n in range(3)], False)


def by_head(body, ins, specs, count, rows, more=(), scratch=()):
    return pl.pallas_call(
        body,
        grid=(HEADS_HERE,),
        out_shape=(jax.ShapeDtypeStruct((count, rows, WIDTH_HERE), jnp.bfloat16),)
        + tuple(jax.ShapeDtypeStruct(shape, jnp.float32) for shape in more),
        in_specs=specs,
        out_specs=(stack_tile(count, rows),) + tuple(fixed(shape) for shape in more),
        scratch_shapes=scratch,
        compiler_params=pltpu.CompilerParams(vmem_limit_bytes=20 * 1024 * 1024),
    )(*ins)


def full_exchange(values, grad_out, query_raw, key_raw, gains, code_row, small, norms):
    def swap(array):
        return lax.all_to_all(array, "seq", split_axis=0, concat_axis=0, tiled=True)

    row = fixed((1, TOK))
    gain_tile = pl.BlockSpec((2, HEAD_DIM), lambda n: (0, n))
    (sent,) = by_head(
        full_pack_body,
        (code_row, values, grad_out, query_raw, key_raw, gains, *norms),
        [row] + [TILE] * 4 + [gain_tile] + [fixed((8, TOK))] * 4,
        5,
        FULL,
    )
    (grads,) = by_head(
        full_attend_body,
        (small, lax.map(swap, sent)),
        [fixed((LANES, LANES)), stack_tile(5, FULL)],
        3,
        FULL,
        scratch=[pltpu.VMEM((FULL, FULL), kind) for kind in (jnp.float32, jnp.bfloat16, jnp.bfloat16)],
    )
    return by_head(
        full_unpack_body,
        (code_row, query_raw, key_raw, gains, lax.map(swap, grads)),
        [row, TILE, TILE, gain_tile, stack_tile(3, FULL)],
        3,
        TOK,
        more=((8, TOK),),
    )


def on_device(
    query_raw, key_raw, values, grad_out, query_gain, key_gain, cluster_of, pair_mask, cluster_owner
):
    own_index = lax.axis_index("seq").astype(jnp.int32)
    z_here = own_index // NR
    gains = jnp.stack([query_gain, key_gain]).astype(jnp.float32)
    table_row, code_row, dest_a, dest_b, flag = prep(cluster_of, cluster_owner, z_here)
    row_sums = jax.ShapeDtypeStruct((8, TOK), jnp.float32)
    norms = over_head(call(squares_body, row_sums)(query_raw, key_raw))
    raw_args = (code_row, values, grad_out, query_raw, key_raw, gains, *norms)

    a_packed = pack(GROUPS_A, NZ, (dest_a, *raw_args))
    a_sent = z_exchange(a_packed, 1)
    (b_packed,) = pack(GROUPS_B, 1, (dest_b, *raw_args))
    b_middle = y_exchange(b_packed)
    small = small_mask(table_row, pair_mask, own_index)

    (a_wide,), (b_wide,) = widths_of(GROUPS_A), widths_of(GROUPS_B)
    (b_blocks,), b_table, flag = spread(
        "z", (b_middle,), (LANES + 4 * b_wide,), Z_CAP, z_here, flag
    )
    b_arrived = z_exchange(b_blocks, 1)
    ((a_rows,),), a_table, flag = spread("y", a_sent, (LANES + 4 * a_wide,), Y_CAP, z_here, flag)
    a_arrived = y_exchange(a_rows)
    (a_grads,) = attend(small, (a_arrived,), a_wide // HEAD_DIM, flag)
    a_back = y_exchange(a_grads)
    b_grads = attend(small, b_arrived, b_wide // HEAD_DIM)
    b_return = z_exchange(b_grads, -1)
    a_blocks = gather(a_table, (a_back,), NZ, Y_CAP, True)
    a_return = z_exchange(a_blocks, -1)
    (b_rows,) = gather(b_table, b_return, 1, Z_CAP, False)
    b_home = y_exchange(b_rows)
    sides = (query_raw, key_raw, gains)
    *home_b, inner_b = unpack(GROUPS_B, dest_b, sides, (b_home,))
    *home_a, inner, overflow = unpack(GROUPS_A, dest_a, sides, a_return, inner_b)
    given = (values, grad_out, query_raw, key_raw, gains, code_row, small, norms)

    def slow(state):
        trip, inputs = lax.optimization_barrier((state[0], given))
        homes, inner = full_exchange(*inputs)
        homes = [homes[n] for n in range(3)]
        return (
            trip + 1.0,
            tuple(h[:, :SPLIT] for h in homes),
            tuple(h[:, SPLIT:] for h in homes),
            inner,
        )

    trips = overflow[0, 0]
    _, home_a, home_b, inner = lax.while_loop(
        lambda state: state[0] < trips,
        slow,
        (jnp.float32(0), tuple(home_a), tuple(home_b), inner),
    )
    inners = over_head(inner)
    out = jax.ShapeDtypeStruct((TOK, WIDTH_HERE), jnp.bfloat16)
    return call(finish_body, (out,) * 3)(*home_a, *home_b, *sides, *norms, *inners)


def solution(mesh):
    return jax.shard_map(
        on_device,
        mesh=mesh,
        in_specs=(
            P("seq", "head"),
            P("seq", "head"),
            P("seq", "head"),
            P("seq", "head"),
            P("head"),
            P("head"),
            P("seq"),
            P(),
            P(),
        ),
        out_specs=(P("seq", "head"), P("seq", "head"), P("seq", "head")),
        check_vma=False,
    )
```

```python
import functools
import math

import jax
import jax.numpy as jnp
from jax import lax
from jax.experimental import pallas as pl
from jax.experimental.pallas import tpu as pltpu
from jax.sharding import PartitionSpec as P


WIDTH = 5120
HEAD_DIM = 128
EPSILON = 1e-06
NEGATIVE = -1e30

TOK = 256
NZ = 8
NR = 8
OWNED = 4
SRC_CAP = 48
Y_CAP = 56
Z_CAP = 56
SRC_ROWS = NZ * SRC_CAP
WIDTH_HERE = 1280
HEADS_HERE = 10
GROUPS_A = ((0, 5),)
GROUPS_B = ((5, 10),)
SPLIT = 5 * HEAD_DIM
LANES = 128


Y_GROUPS = [[NR * z + r for r in range(NR)] for z in range(NZ)]


def z_perm(shift):
    return [(s, ((s // NR + shift) % NZ) * NR + s % NR) for s in range(NZ * NR)]


def head_perm(shift):
    return [(s, (s + shift) % 4) for s in range(4)]


def call(body, out_shape, flops=0, moved=0, scratch=()):
    return pl.pallas_call(
        body,
        out_shape=out_shape,
        scratch_shapes=scratch,
        cost_estimate=pl.CostEstimate(flops=flops, bytes_accessed=moved, transcendentals=0),
        compiler_params=pltpu.CompilerParams(vmem_limit_bytes=20 * 1024 * 1024),
    )


def iota(shape, dim):
    return lax.broadcasted_iota(jnp.int32, shape, dim)


def to_col(row):
    n = row.shape[1]
    eye = iota((n, n), 0) == iota((n, n), 1)
    return jnp.sum(jnp.where(eye, jnp.broadcast_to(row, (n, n)), jnp.zeros((), row.dtype)), axis=1, keepdims=True)


def to_row(col):
    n = col.shape[0]
    eye = iota((n, n), 0) == iota((n, n), 1)
    return jnp.sum(jnp.where(eye, jnp.broadcast_to(col, (n, n)), jnp.zeros((), col.dtype)), axis=0, keepdims=True)


def mm(a, b, dims):
    return lax.dot_general(a, b, (dims, ((), ())), preferred_element_type=jnp.float32)


def prep_body(cluster_ref, owner_ref, z_ref, table_ref, code_ref, dest_a_ref, dest_b_ref, flag_ref):
    square = (TOK, TOK)
    owner_row = owner_ref[...]
    owner_col = to_col(owner_row)
    earlier = iota(square, 0) < iota(square, 1)
    one, zero = jnp.int32(1), jnp.int32(0)
    local_row = jnp.sum(
        jnp.where((owner_col == owner_row) & earlier, one, zero), axis=0, keepdims=True
    )
    table_row = owner_row * OWNED + local_row
    table_ref[...] = table_row
    table_col = to_col(table_row)
    code_row = jnp.sum(
        jnp.where(iota(square, 0) == cluster_ref[...], table_col, zero), axis=0, keepdims=True
    )
    code_ref[...] = code_row
    ranks = []
    for key_row, out_ref in (
        (((code_row >> 5) - z_ref[0] + NZ) & (NZ - 1), dest_a_ref),
        ((code_row >> 2) & (NR - 1), dest_b_ref),
    ):
        key_col = to_col(key_row)
        rank_row = jnp.sum(
            jnp.where((key_col == key_row) & earlier, one, zero), axis=0, keepdims=True
        )
        out_ref[...] = jnp.where(rank_row < SRC_CAP, key_row * SRC_CAP + rank_row, -1)
        ranks.append(rank_row)
    most = jnp.max(jnp.maximum(ranks[0], ranks[1]), axis=1, keepdims=True)
    flag_ref[...] = jnp.broadcast_to(jnp.where(most < SRC_CAP, 0.0, 1.0), (1, LANES))


FLAG = jax.ShapeDtypeStruct((1, LANES), jnp.float32)
VMEM_SPEC = pl.BlockSpec(memory_space=pltpu.VMEM)
SMEM_SPEC = pl.BlockSpec(memory_space=pltpu.SMEM)


def prep(cluster_of, cluster_owner, z_here):
    row = jax.ShapeDtypeStruct((1, TOK), jnp.int32)
    return pl.pallas_call(
        prep_body,
        out_shape=(row,) * 4 + (FLAG,),
        in_specs=[VMEM_SPEC, VMEM_SPEC, SMEM_SPEC],
        out_specs=(VMEM_SPEC,) * 5,
        name="prep",
    )(cluster_of.reshape(1, TOK), cluster_owner.reshape(1, TOK), z_here.reshape(1))


def mask_body(table_ref, mask_ref, own_ref, out_ref):
    slots = iota((LANES, TOK), 0)
    chosen = (table_ref[...] == own_ref[0] * OWNED + slots) & (slots < OWNED)
    chosen = jnp.where(chosen, 1.0, 0.0).astype(jnp.bfloat16)
    pairs = mask_ref[...].astype(jnp.float32).astype(jnp.bfloat16)
    rows = mm(chosen, pairs, ((1,), (0,))).astype(jnp.bfloat16)
    out_ref[...] = mm(rows, chosen, ((1,), (1,))).astype(jnp.bfloat16)


def small_mask(table_row, pair_mask, own_index):
    return pl.pallas_call(
        mask_body,
        out_shape=jax.ShapeDtypeStruct((LANES, LANES), jnp.bfloat16),
        in_specs=[VMEM_SPEC, VMEM_SPEC, SMEM_SPEC],
        out_specs=VMEM_SPEC,
        name="mask",
    )(table_row, pair_mask, own_index.reshape(1))


def bias_of(code, small):
    local = jnp.where(code > 0, (code - 1) & (OWNED - 1), -1)
    hot = jnp.where(local == iota(local.shape, 1), 1.0, 0.0).astype(jnp.bfloat16)
    reach = mm(hot, small, ((1,), (1,))).astype(jnp.bfloat16)
    return jnp.where(mm(reach, hot, ((1,), (1,))) > 0.5, 0.0, NEGATIVE)


def squares_body(q_ref, k_ref, out_ref):
    q = q_ref[...].astype(jnp.float32)
    k = k_ref[...].astype(jnp.float32)
    out_ref[0:1, :] = to_row(jnp.sum(q * q, axis=1, keepdims=True))
    out_ref[1:2, :] = to_row(jnp.sum(k * k, axis=1, keepdims=True))
    out_ref[2:8, :] = jnp.zeros((6, TOK), jnp.float32)


def over_head(part):
    return [part] + [lax.ppermute(part, "head", head_perm(d)) for d in (1, 2, 3)]


def total_of(refs):
    return (refs[0][...] + refs[1][...]) + (refs[2][...] + refs[3][...])


def scale_col(total, which):
    return jnp.sqrt(to_col(total[which : which + 1, :]) / WIDTH + EPSILON)


def place_rows(dest_row):
    return jnp.where(iota((SRC_ROWS, TOK), 0) == dest_row, 1.0, 0.0).astype(jnp.bfloat16)


def store_blocks(outs, packed, start):
    width = packed.shape[1]
    cap = packed.shape[0] // len(outs)
    for d, out in enumerate(outs):
        out[:, start : start + width] = packed[d * cap : (d + 1) * cap, :]


def normed(raw, gain, inverse):
    return (raw.astype(jnp.float32) * gain.astype(jnp.float32) * inverse).astype(jnp.bfloat16)


def widths_of(groups):
    return [(hi - lo) * HEAD_DIM for lo, hi in groups]


def pack_body(groups, dest_ref, code_ref, v_ref, g_ref, q_ref, k_ref, gain_ref, *refs):
    total = total_of(refs[:4])
    outs = refs[4:]
    hot = place_rows(dest_ref[...])
    at = 0

    def put(part):
        store_blocks(outs, mm(hot, part, ((1,), (0,))).astype(jnp.bfloat16), at)
        return at + part.shape[1]

    code = jnp.broadcast_to(to_col(code_ref[...]) + 1, (TOK, LANES))
    at = put(code.astype(jnp.float32).astype(jnp.bfloat16))
    sides = [
        (ref, gain, 1.0 / scale_col(total, which))
        for which, (ref, gain) in enumerate(((q_ref, gain_ref[...][0:1]), (k_ref, gain_ref[...][1:2])))
    ]
    for lo, hi in groups:
        cols = slice(0, (hi - lo) * HEAD_DIM)
        at = put(v_ref[:, cols])
        at = put(g_ref[:, cols])
        for ref, gain, scale in sides:
            at = put(normed(ref[:, cols], gain[:, cols], scale))


def blocks_of(count, rows, width):
    return (jax.ShapeDtypeStruct((rows, width), jnp.bfloat16),) * count


def whole_spec(shape):
    return pl.BlockSpec(shape, lambda n: (0,) * len(shape))


def half_call(body, out_shape, groups, args, sliced, flops):
    ((lo, hi),) = groups
    width = (hi - lo) * HEAD_DIM
    half = lo // (hi - lo)
    specs = [
        pl.BlockSpec((x.shape[0], width), lambda n: (0, half)) if i in sliced else whole_spec(x.shape)
        for i, x in enumerate(args)
    ]
    return pl.pallas_call(
        body,
        grid=(1,),
        out_shape=out_shape,
        in_specs=specs,
        out_specs=tuple(whole_spec(x.shape) for x in out_shape),
        cost_estimate=pl.CostEstimate(flops=flops, bytes_accessed=0, transcendentals=0),
        compiler_params=pltpu.CompilerParams(vmem_limit_bytes=20 * 1024 * 1024),
    )(*args)


def pack(groups, count, args):
    width = sum(widths_of(groups)) * 4 + LANES
    return half_call(
        functools.partial(pack_body, groups),
        blocks_of(count, SRC_ROWS // count, width),
        groups,
        args,
        range(2, 7),
        2 * SRC_ROWS * TOK * width,
    )


FAR = (4, 3, 5)
NEAR = (2, 6, 1, 7)


def z_exchange(blocks, sign):
    got = {0: blocks[0]}
    for shifts in (FAR, NEAR):
        for d in shifts:
            got[d] = lax.ppermute(blocks[d], "seq", z_perm(sign * d))
    return [got[d] for d in range(NZ)]


def y_exchange(rows):
    return lax.all_to_all(
        rows, "seq", split_axis=0, concat_axis=0, axis_index_groups=Y_GROUPS, tiled=True
    )


def stacked(blocks, cols):
    if len(blocks) == 1:
        return blocks[0][:, cols]
    return jnp.concatenate([b[:, cols] for b in blocks], axis=0)


def steps_of(width):
    return [slice(a, min(a + 512, width)) for a in range(0, width, 512)]


def spread_body(mode, count_in, cap, z_ref, seen_ref, *refs):
    blocks, outs, table_ref, flag_ref = refs[:count_in], refs[count_in:-2], refs[-2], refs[-1]
    code = stacked(blocks, slice(0, LANES)).astype(jnp.float32).astype(jnp.int32)[:, 0:1]
    if mode == "y":
        key = ((code - 1) >> 2) & (NR - 1)
    else:
        key = (((code - 1) >> 5) - z_ref[0] + NZ) & (NZ - 1)
    key_col = jnp.where(code > 0, key, -1)
    key_row = to_row(key_col)
    square = (SRC_ROWS, SRC_ROWS)
    before = (key_col == key_row) & (iota(square, 0) < iota(square, 1))
    rank_row = jnp.sum(jnp.where(before, jnp.int32(1), jnp.int32(0)), axis=0, keepdims=True)
    dest = jnp.where((key_row >= 0) & (rank_row < cap), key_row * cap + rank_row, -1)
    table_ref[...] = dest
    most = jnp.max(jnp.where(key_row >= 0, rank_row, 0), axis=1, keepdims=True)
    flag_ref[...] = jnp.maximum(seen_ref[...], jnp.where(most < cap, 0.0, 1.0))
    hot = jnp.where(iota((NZ * cap, SRC_ROWS), 0) == dest, 1.0, 0.0).astype(jnp.bfloat16)
    per = 1 if mode == "y" else NZ
    start = 0
    for n in range(0, len(outs), per):
        group = outs[n : n + per]
        width = group[0].shape[1]
        for cols in steps_of(width):
            rows = stacked(blocks, slice(start + cols.start, start + cols.stop))
            store_blocks(group, mm(hot, rows, ((1,), (0,))).astype(jnp.bfloat16), cols.start)
        start += width


def spread(mode, blocks, widths, cap, z_here, seen):
    per = 1 if mode == "y" else NZ
    shapes = sum((blocks_of(per, NZ * cap // per, width) for width in widths), ())
    outs = pl.pallas_call(
        functools.partial(spread_body, mode, len(blocks), cap),
        out_shape=shapes + (jax.ShapeDtypeStruct((1, SRC_ROWS), jnp.int32), FLAG),
        in_specs=[SMEM_SPEC] + [VMEM_SPEC] * (len(blocks) + 1),
        out_specs=(VMEM_SPEC,) * (len(shapes) + 2),
        cost_estimate=pl.CostEstimate(
            flops=2 * NZ * cap * SRC_ROWS * sum(widths), bytes_accessed=0, transcendentals=0
        ),
        compiler_params=pltpu.CompilerParams(vmem_limit_bytes=20 * 1024 * 1024),
    )(z_here.reshape(1), seen, *blocks)
    return [outs[n * per : (n + 1) * per] for n in range(len(widths))], outs[-2], outs[-1]


def gather_body(count, cap, flagged, table_ref, *refs):
    blocks, outs = refs[:count], refs[count:]
    hot = jnp.where(iota((NZ * cap, SRC_ROWS), 0) == table_ref[...], 1.0, 0.0).astype(jnp.bfloat16)
    base = 0
    if flagged:
        base = LANES
        seen = jnp.max(stacked(blocks, slice(0, LANES)).astype(jnp.float32), axis=0, keepdims=True)
        flags = jnp.broadcast_to(seen, (SRC_ROWS, LANES)).astype(jnp.bfloat16)
        store_blocks(outs, flags, 0)
    for cols in steps_of(outs[0].shape[1] - base):
        cols = slice(base + cols.start, base + cols.stop)
        packed = mm(hot, stacked(blocks, cols), ((0,), (0,))).astype(jnp.bfloat16)
        store_blocks(outs, packed, cols.start)


def gather(table, blocks, count_out, cap, flagged):
    width = blocks[0].shape[1]
    return call(
        functools.partial(gather_body, len(blocks), cap, flagged),
        blocks_of(count_out, SRC_ROWS // count_out, width),
        flops=2 * NZ * cap * SRC_ROWS * width,
        moved=4 * NZ * cap * width,
    )(table, *blocks)


def inner_row(grad, raw, gain):
    lifted = grad.astype(jnp.float32) * gain.astype(jnp.float32)
    return to_row(jnp.sum(lifted * raw.astype(jnp.float32), axis=1, keepdims=True))


def unpack_body(groups, flagged, dest_ref, q_ref, k_ref, gain_ref, *refs):
    if flagged:
        other_ref, flag_ref, refs = refs[0], refs[-1], refs[1:-1]
    blocks, outs, inner_ref = refs[:-4], refs[-4:-1], refs[-1]
    hot = place_rows(dest_ref[...])
    sides = (None, (q_ref, gain_ref[...][0:1]), (k_ref, gain_ref[...][1:2]))
    at = 0
    if flagged:
        at = LANES
        inner_ref[...] = other_ref[...]
        seen = [jnp.max(b[:, :LANES].astype(jnp.float32), axis=0, keepdims=True) for b in blocks]
        flag_ref[...] = functools.reduce(jnp.maximum, seen)
    else:
        inner_ref[...] = jnp.zeros((8, TOK), jnp.float32)
    for lo, hi in groups:
        width = (hi - lo) * HEAD_DIM
        cols = slice(lo * HEAD_DIM, hi * HEAD_DIM)
        base = (lo - groups[0][0]) * HEAD_DIM
        for n, (out, side) in enumerate(zip(outs, sides)):
            grad = mm(hot, stacked(blocks, slice(at, at + width)), ((0,), (0,))).astype(jnp.bfloat16)
            at += width
            out[:, base : base + width] = grad
            if side is not None:
                inner_ref[n - 1 : n, :] += inner_row(grad, side[0][:, cols], side[1][:, cols])


def unpack(groups, dest, sides, blocks, other=None):
    width = sum(widths_of(groups))
    flagged = other is not None
    return call(
        functools.partial(unpack_body, groups, flagged),
        blocks_of(3, TOK, width)
        + (jax.ShapeDtypeStruct((8, TOK), jnp.float32),)
        + ((FLAG,) if flagged else ()),
        flops=2 * SRC_ROWS * TOK * width * 3,
        moved=4 * SRC_ROWS * width * 3,
    )(dest, *sides, *((other,) if flagged else ()), *blocks)


def at_head(start, h):
    return pl.ds(pl.multiple_of(start + h * HEAD_DIM, HEAD_DIM), HEAD_DIM)


def one_head(v_ref, g_ref, q_ref, k_ref, bias_ref, probs_ref, grads_ref, outs, unroll):
    rows = bias_ref.shape[0]
    inv = 1.0 / math.sqrt(HEAD_DIM)

    def one_part(part):
        scores = mm(k_ref[...], q_ref[part, :], ((1,), (1,))) * inv + bias_ref[:, part]
        raised = jnp.exp(scores - jnp.max(scores, axis=0, keepdims=True))
        probs = raised * (1.0 / jnp.sum(raised, axis=0, keepdims=True))
        low = probs.astype(jnp.bfloat16)
        gp = mm(v_ref[...], g_ref[part, :], ((1,), (1,)))
        delta = jnp.sum(low.astype(jnp.float32) * gp, axis=0, keepdims=True)
        probs_ref[:, part] = low
        grads_ref[:, part] = (probs * (gp - delta) * inv).astype(jnp.bfloat16)

    if unroll:
        for a in range(0, rows, LANES):
            one_part(slice(a, min(a + LANES, rows)))
    else:

        def step(n, carry):
            one_part(pl.ds(pl.multiple_of(n * LANES, LANES), LANES))
            return carry

        lax.fori_loop(0, rows // LANES, step, 0)
    gs = grads_ref[...]
    outs[0][...] = mm(probs_ref[...], g_ref[...], ((1,), (0,))).astype(jnp.bfloat16)
    outs[1][...] = mm(gs, k_ref[...], ((0,), (0,))).astype(jnp.bfloat16)
    outs[2][...] = mm(gs, q_ref[...], ((1,), (0,))).astype(jnp.bfloat16)


def attend_body(heads, count, flagged, mask_ref, *refs):
    if flagged:
        flag_ref, refs = refs[0], refs[1:]
    blocks, outs = refs[:count], refs[count : 2 * count]
    bias_ref, probs_ref, grads_ref = refs[2 * count : 2 * count + 3]
    rows, width = bias_ref.shape[0], heads * HEAD_DIM
    base = LANES if flagged else 0
    if count == 1:
        data, result = blocks[0], outs[0]
    else:
        data, result = refs[2 * count + 3 :]
        cap = rows // count
        for d, block in enumerate(blocks):
            data[d * cap : (d + 1) * cap, :] = block[...]
    bias_ref[...] = bias_of(data[:, :LANES].astype(jnp.float32).astype(jnp.int32), mask_ref[...])
    if flagged:
        result[:, :LANES] = jnp.broadcast_to(flag_ref[...], (rows, LANES)).astype(jnp.bfloat16)

    def step(h, carry):
        ins = [data.at[:, at_head(LANES + n * width, h)] for n in range(4)]
        grads = [result.at[:, at_head(base + n * width, h)] for n in range(3)]
        one_head(*ins, bias_ref, probs_ref, grads_ref, grads, True)
        return carry

    lax.fori_loop(0, heads, step, 0)
    if count > 1:
        store_blocks(outs, result[...], 0)


def attend(mask, blocks, heads, flag=None):
    count = len(blocks)
    rows = count * blocks[0].shape[0]
    flagged = flag is not None
    width = 3 * heads * HEAD_DIM + (LANES if flagged else 0)
    square = (rows, rows)
    scratch = [pltpu.VMEM(square, kind) for kind in (jnp.float32, jnp.bfloat16, jnp.bfloat16)]
    if count > 1:
        scratch.append(pltpu.VMEM((rows, blocks[0].shape[1]), jnp.bfloat16))
        scratch.append(pltpu.VMEM((rows, width), jnp.bfloat16))
    return call(
        functools.partial(attend_body, heads, count, flagged),
        blocks_of(count, rows // count, width),
        flops=20 * rows * rows * HEAD_DIM * heads,
        moved=14 * rows * heads * HEAD_DIM,
        scratch=scratch,
    )(mask, *((flag,) if flagged else ()), *blocks)


def finish_body(*refs):
    va, qa, ka, vb, qb, kb, q_ref, k_ref, gain_ref = refs[:9]
    squares = total_of(refs[9:13])
    inners = total_of(refs[13:17])
    gq_ref, gk_ref, gv_ref = refs[17:]
    spans = (slice(0, SPLIT), slice(SPLIT, WIDTH_HERE))
    sides = (((qa, qb), q_ref, gq_ref), ((ka, kb), k_ref, gk_ref))
    for n, (pieces, x, out) in enumerate(sides):
        scale = scale_col(squares, n)
        inner = to_col(inners[n : n + 1, :])
        slope = inner / (WIDTH * scale * scale * scale)
        inverse = 1.0 / scale
        for piece, cols in zip(pieces, spans):
            lifted = piece[...].astype(jnp.float32) * gain_ref[...][n : n + 1, cols]
            result = lifted * inverse - x[:, cols].astype(jnp.float32) * slope
            out[:, cols] = result.astype(jnp.bfloat16)
    for piece, cols in zip((va, vb), spans):
        gv_ref[:, cols] = piece[...]


FULL = 64 * OWNED * 2
TILE = pl.BlockSpec((TOK, HEAD_DIM), lambda n: (0, n))


def fixed(shape):
    return pl.BlockSpec(shape, lambda n: (0, 0))


def stack_tile(count, rows):
    return pl.BlockSpec((count, rows, HEAD_DIM), lambda n: (0, 0, n))


def full_slots(code_ref):
    code_row = code_ref[...]
    square = (TOK, TOK)
    same = (to_col(code_row) == code_row) & (iota(square, 0) < iota(square, 1))
    rank = jnp.sum(jnp.where(same, jnp.int32(1), jnp.int32(0)), axis=0, keepdims=True)
    return jnp.where(iota((FULL, TOK), 0) == code_row * 2 + rank, 1.0, 0.0).astype(jnp.bfloat16)


def full_pack_body(code_ref, v_ref, g_ref, q_ref, k_ref, gain_ref, *refs):
    total, out_ref = total_of(refs[:4]), refs[4]
    parts = [v_ref[...], g_ref[...]]
    for n, ref in enumerate((q_ref, k_ref)):
        parts.append(normed(ref[...], gain_ref[...][n : n + 1], 1.0 / scale_col(total, n)))
    parts.append(jnp.ones((TOK, HEAD_DIM), jnp.bfloat16))
    packed = mm(full_slots(code_ref), jnp.concatenate(parts, axis=1), ((1,), (0,))).astype(jnp.bfloat16)
    for n in range(5):
        out_ref[n] = packed[:, n * HEAD_DIM : (n + 1) * HEAD_DIM]


def full_unpack_body(code_ref, q_ref, k_ref, gain_ref, in_ref, out_ref, inner_ref):
    rows = jnp.concatenate([in_ref[n] for n in range(3)], axis=1)
    grads = mm(full_slots(code_ref), rows, ((0,), (0,))).astype(jnp.bfloat16)

    @pl.when(pl.program_id(0) == 0)
    def _():
        inner_ref[...] = jnp.zeros((8, TOK), jnp.float32)

    for n, ref in enumerate((None, q_ref, k_ref)):
        grad = grads[:, n * HEAD_DIM : (n + 1) * HEAD_DIM]
        out_ref[n] = grad
        if n > 0:
            lifted = grad.astype(jnp.float32) * gain_ref[...][n - 1 : n]
            part = jnp.sum(lifted * ref[...].astype(jnp.float32), axis=1, keepdims=True)
            inner_ref[n - 1 : n, :] += to_row(part)


def full_attend_body(mask_ref, in_ref, out_ref, bias_ref, probs_ref, grads_ref):
    @pl.when(pl.program_id(0) == 0)
    def _():
        live = in_ref[4].astype(jnp.float32) > 0.5
        bias_ref[...] = bias_of(jnp.where(live, ((iota((FULL, LANES), 0) >> 1) & 3) + 1, 0), mask_ref[...])

    one_head(*(in_ref.at[n] for n in range(4)), bias_ref, probs_ref, grads_ref, [out_ref.at[n] for n in range(3)], False)


def by_head(body, ins, specs, count, rows, more=(), scratch=()):
    return pl.pallas_call(
        body,
        grid=(HEADS_HERE,),
        out_shape=(jax.ShapeDtypeStruct((count, rows, WIDTH_HERE), jnp.bfloat16),)
        + tuple(jax.ShapeDtypeStruct(shape, jnp.float32) for shape in more),
        in_specs=specs,
        out_specs=(stack_tile(count, rows),) + tuple(fixed(shape) for shape in more),
        scratch_shapes=scratch,
        compiler_params=pltpu.CompilerParams(vmem_limit_bytes=20 * 1024 * 1024),
    )(*ins)


def full_exchange(values, grad_out, query_raw, key_raw, gains, code_row, small, norms):
    def swap(array):
        return lax.all_to_all(array, "seq", split_axis=0, concat_axis=0, tiled=True)

    row = fixed((1, TOK))
    gain_tile = pl.BlockSpec((2, HEAD_DIM), lambda n: (0, n))
    (sent,) = by_head(
        full_pack_body,
        (code_row, values, grad_out, query_raw, key_raw, gains, *norms),
        [row] + [TILE] * 4 + [gain_tile] + [fixed((8, TOK))] * 4,
        5,
        FULL,
    )
    (grads,) = by_head(
        full_attend_body,
        (small, lax.map(swap, sent)),
        [fixed((LANES, LANES)), stack_tile(5, FULL)],
        3,
        FULL,
        scratch=[pltpu.VMEM((FULL, FULL), kind) for kind in (jnp.float32, jnp.bfloat16, jnp.bfloat16)],
    )
    return by_head(
        full_unpack_body,
        (code_row, query_raw, key_raw, gains, lax.map(swap, grads)),
        [row, TILE, TILE, gain_tile, stack_tile(3, FULL)],
        3,
        TOK,
        more=((8, TOK),),
    )


def on_device(
    query_raw, key_raw, values, grad_out, query_gain, key_gain, cluster_of, pair_mask, cluster_owner
):
    own_index = lax.axis_index("seq").astype(jnp.int32)
    z_here = own_index // NR
    gains = jnp.stack([query_gain, key_gain]).astype(jnp.float32)
    table_row, code_row, dest_a, dest_b, flag = prep(cluster_of, cluster_owner, z_here)
    row_sums = jax.ShapeDtypeStruct((8, TOK), jnp.float32)
    norms = over_head(call(squares_body, row_sums)(query_raw, key_raw))
    raw_args = (code_row, values, grad_out, query_raw, key_raw, gains, *norms)

    a_packed = pack(GROUPS_A, NZ, (dest_a, *raw_args))
    a_sent = z_exchange(a_packed, 1)
    (b_packed,) = pack(GROUPS_B, 1, (dest_b, *raw_args))
    b_middle = y_exchange(b_packed)
    small = small_mask(table_row, pair_mask, own_index)

    (a_wide,), (b_wide,) = widths_of(GROUPS_A), widths_of(GROUPS_B)
    (b_blocks,), b_table, flag = spread(
        "z", (b_middle,), (LANES + 4 * b_wide,), Z_CAP, z_here, flag
    )
    b_arrived = z_exchange(b_blocks, 1)
    ((a_rows,),), a_table, flag = spread("y", a_sent, (LANES + 4 * a_wide,), Y_CAP, z_here, flag)
    a_arrived = y_exchange(a_rows)
    (a_grads,) = attend(small, (a_arrived,), a_wide // HEAD_DIM, flag)
    a_back = y_exchange(a_grads)
    b_grads = attend(small, b_arrived, b_wide // HEAD_DIM)
    b_return = z_exchange(b_grads, -1)
    a_blocks = gather(a_table, (a_back,), NZ, Y_CAP, True)
    a_return = z_exchange(a_blocks, -1)
    (b_rows,) = gather(b_table, b_return, 1, Z_CAP, False)
    b_home = y_exchange(b_rows)
    sides = (query_raw, key_raw, gains)
    *home_b, inner_b = unpack(GROUPS_B, dest_b, sides, (b_home,))
    *home_a, inner, overflow = unpack(GROUPS_A, dest_a, sides, a_return, inner_b)
    given = (values, grad_out, query_raw, key_raw, gains, code_row, small, norms)

    def slow(state):
        trip, inputs = lax.optimization_barrier((state[0], given))
        homes, inner = full_exchange(*inputs)
        homes = [homes[n] for n in range(3)]
        return (
            trip + 1.0,
            tuple(h[:, :SPLIT] for h in homes),
            tuple(h[:, SPLIT:] for h in homes),
            inner,
        )

    trips = overflow[0, 0]
    _, home_a, home_b, inner = lax.while_loop(
        lambda state: state[0] < trips,
        slow,
        (jnp.float32(0), tuple(home_a), tuple(home_b), inner),
    )
    inners = over_head(inner)
    out = jax.ShapeDtypeStruct((TOK, WIDTH_HERE), jnp.bfloat16)
    return call(finish_body, (out,) * 3)(*home_a, *home_b, *sides, *norms, *inners)


def solution(mesh):
    return jax.shard_map(
        on_device,
        mesh=mesh,
        in_specs=(
            P("seq", "head"),
            P("seq", "head"),
            P("seq", "head"),
            P("seq", "head"),
            P("head"),
            P("head"),
            P("seq"),
            P(),
            P(),
        ),
        out_specs=(P("seq", "head"), P("seq", "head"), P("seq", "head")),
        check_vma=False,
    )
```
